32 devices in a mesh: section: 4 (over y, x), dev: 8 (over z, core).
Axes of the slice: x: 2, y: 2, z: 4, core: 2. Of those that a mesh axis runs over, the one named last changes fastest.
Arguments:
- hidden: bfloat16 [256, 2048], P('dev'), may hold values from -8 to 8
- lengths: int32 [256], P('dev'), may hold values from 1 to 256, as said below
- attn_gain: float32 [2048], replicated, may hold values from 0.1 to 1.9
- w_query: bfloat16 [2048, 3072], P(None, 'section'), may hold values from -0.125 to 0.125
- w_latent: bfloat16 [2048, 512], replicated, may hold values from -0.125 to 0.125
- latent_gain: float32 [512], replicated, may hold values from 0.1 to 1.9
- w_rope_key: bfloat16 [64, 2048], replicated, may hold values from -0.125 to 0.125
- w_key_up: bfloat16 [16, 512, 128], P('section'), may hold values from -0.5 to 0.5
- w_value_up: bfloat16 [16, 512, 128], P('section'), may hold values from -0.25 to 0.25
- w_out: bfloat16 [2048, 2048], P('section'), may hold values from -0.125 to 0.125
- latent_cache: bfloat16 [256, 256, 512], P('dev'), may hold values from -6 to 6
- rope_cache: bfloat16 [256, 64, 256], P('dev'), may hold values from -1200 to 1200
- ffn_gain: float32 [2048], replicated, may hold values from 0.1 to 1.9
- expert_ids: int32 [256, 6], P('dev'), may hold values from 0 to 63, all different within a row; in each aligned block of 8 rows (0 to 7, 8 to 15, ...) at most 2 rows name the same one
- route_weights: float32 [256, 6], P('dev'), may hold values from 0.05 to 0.5
- w_gate_up: bfloat16 [64, 2, 1408, 2048], P('dev', None, 'section'), may hold values from -0.125 to 0.125
- w_down: bfloat16 [64, 1408, 2048], P('dev', 'section'), may hold values from -0.15625 to 0.15625
Outputs:
- layer_out: bfloat16 [256, 2048], P('dev')
The draws below stay inside these ranges and needn't reach their ends.
Inputs may be any that keep to these rules, and one draw needn't show every extreme that they name: `lengths`: every aligned block of 32 rows holds a row of length 256. `expert_ids`: each row names 6 different experts. In every aligned block of 8 rows no expert is named by more than 2 rows, and some block has an expert named by exactly 2.
All inputs are finite; a program needn't handle non-finite values.
Results may differ from the reference program's by a relative error of at most 0.011.
Values may be sent and summed in bfloat16 or wider, within the bound.
A program may use at most 128 MiB of HBM per device.

```python
import math
import jax
import jax.numpy as jnp
import numpy as np
from jax import lax

D = 2048
HEADS = 16
NOPE = 128
ROPE = 64
LATENT = 512
VHEAD = 128
FF = 1408
EXPERTS = 64
TOPK = 6
ROW_DEV = 32
LEN = 256
MOST = 2
ROWS = 256
ROW_Q = 8


def draw_hidden(key, part):
    base_key, row_key, column_key = jax.random.split(jax.random.fold_in(key, 11), 3)
    row_scale = jnp.exp(jax.random.uniform(row_key, (ROWS, 1), jnp.float32, math.log(0.2), math.log(2.0)))
    column_scale = jnp.exp(jax.random.uniform(column_key, (1, D), jnp.float32, math.log(0.3), math.log(3.0)))
    values = jax.random.normal(base_key, (ROWS, D), jnp.float32)
    return jnp.clip(values * row_scale * column_scale, -8.0, 8.0).astype(jnp.bfloat16)


def draw_lengths(key, part):
    length_key, pick_key = jax.random.split(jax.random.fold_in(key, 23))
    values = jax.random.randint(length_key, (ROWS,), 1, LEN + 1, dtype=jnp.int32)
    chosen = jax.random.randint(pick_key, (ROWS // ROW_DEV,), 0, ROW_DEV, dtype=jnp.int32)
    positions = jnp.arange(ROWS, dtype=jnp.int32)
    full_row = positions % ROW_DEV == chosen[positions // ROW_DEV]
    return jnp.where(full_row, LEN, values).astype(jnp.int32)


def draw_rope_cache(key, part):
    base_key = jax.random.fold_in(jax.random.fold_in(key, 37), 0)
    values = jnp.clip(jax.random.normal(base_key, (ROWS, ROPE, LEN), jnp.float32), -6.0, 6.0)
    return jnp.clip(values, -1200.0, 1200.0).astype(jnp.bfloat16)


def steps_of(rng, extent, cuts, low, top_value):
    level = 1.0
    for dim, blocks in cuts:
        draws = jax.random.uniform(jax.random.fold_in(jax.random.fold_in(rng, 6), dim), (blocks,), jnp.float32, low / len(cuts), top_value / len(cuts))
        level = level * jnp.repeat(jnp.exp(draws), extent[dim] // blocks).reshape((-1,) + (1,) * (len(extent) - 1 - dim))
    return level


def routed_block(stream_key, own, number, rows, number_of, top, limit, lean):
    ranking = jax.random.permutation(stream_key, number_of)
    heavy_load, usual = load_shares(number_of, rows * top, limit, lean, True), load_shares(number_of, rows * top, limit, lean, False)
    places = jnp.arange(number_of)

    def named(sizes, turn):
        used = int((sizes > 0).sum())
        fixed = max(1, used // 4)
        passed = fixed + (places - fixed + turn * (used - fixed)) % max(1, number_of - fixed)
        return jnp.zeros((number_of,), jnp.int32).at[ranking[jnp.where(places < fixed, places, passed)]].set(jnp.asarray(sizes, jnp.int32))

    sizes = jnp.where(number % 4 == 0, named(heavy_load, number // 4), named(usual, number - number // 4 - 1))
    mixed = jax.random.permutation(jax.random.fold_in(own, 3), number_of)
    donor, taker = mixed[0:number_of // 2 * 2:2], mixed[1:number_of // 2 * 2:2]
    slack = jnp.minimum(sizes[donor] - 1, limit - sizes[taker]) // 2
    slack = jnp.where((donor == ranking[0]) | (taker == ranking[0]) | (sizes[taker] == 0), 0, jnp.maximum(slack, 0))
    passed = jax.random.randint(jax.random.fold_in(own, 4), (number_of // 2,), 0, 1 << 20) % (slack + 1)
    sizes = sizes.at[donor].add(-passed).at[taker].add(passed)
    items = jnp.searchsorted(jnp.cumsum(sizes), jnp.arange(rows * top), side="right").astype(jnp.int32)
    grid = items.reshape(top, rows).T
    grid = grid[jax.random.permutation(jax.random.fold_in(own, 1), rows)]
    turn = jax.random.randint(jax.random.fold_in(own, 2), (rows, 1), 0, top)
    return jnp.take_along_axis(grid, (jnp.arange(top)[None, :] + turn) % top, axis=1)


def load_shares(amount, total, bound, lean, full):
    weights = [(1 << 20) // math.isqrt(rank ** lean) + 1 for rank in range(1, amount + 1)]
    largest = bound if full else min(bound, max(-(-total // amount), total * weights[0] // sum(weights)))
    least = 1 if total - largest >= amount - 1 else 0
    holding, spare = [largest] + [least] * (amount - 1), total - largest - least * (amount - 1)
    while spare > 0:
        free = [i for i in range(1, amount) if holding[i] < largest] or [i for i in range(1, amount) if holding[i] < bound]
        mass, budget = sum([weights[i] for i in free]), spare
        for i in free:
            more = min(bound - holding[i], max(1, budget * weights[i] // mass), spare)
            holding[i] = holding[i] + more
            spare = spare - more
    return np.array(holding)


def gaussian(stream_key, extent, deviation, reach, cuts=(), held_as=jnp.bfloat16):
    array = deviation * jax.random.normal(stream_key, extent, jnp.float32)
    if cuts:
        array = array * steps_of(stream_key, extent, cuts, -0.22, 0.18)
    return jnp.clip(array, -reach, reach).astype(held_as)


def setup_inputs(seed: int = 0) -> dict:
    splits = jax.random.split(jax.random.key(seed), 18)
    hidden = draw_hidden(jax.random.fold_in(splits[17], 71), 0)
    lengths = draw_lengths(jax.random.fold_in(splits[17], 71), 0)
    attn_gain = jnp.clip(1.0 + 0.18 * jax.random.normal(splits[2], (D,), jnp.float32), 0.1, 1.9)
    w_query = gaussian(splits[3], (D, HEADS * (NOPE + ROPE)), D ** -0.5, 0.125, ((1, 4),))
    w_latent = gaussian(splits[4], (D, LATENT), D ** -0.5, 0.125)
    latent_gain = jnp.clip(1.0 + 0.18 * jax.random.normal(splits[5], (LATENT,), jnp.float32), 0.1, 1.9)
    w_rope_key = gaussian(splits[6], (ROPE, D), D ** -0.5, 0.125)
    w_key_up = gaussian(splits[7], (HEADS, LATENT, NOPE), NOPE ** -0.5, 0.5, ((0, 4),))
    w_value_up = gaussian(splits[8], (HEADS, LATENT, VHEAD), LATENT ** -0.5, 0.25, ((0, 4),))
    w_out = gaussian(splits[9], (HEADS * VHEAD, D), (HEADS * VHEAD) ** -0.5, 0.125, ((0, 4),))
    latent_cache = gaussian(splits[10], (ROWS, LEN, LATENT), 1.0, 6.0, ((0, 8),))
    rope_cache = draw_rope_cache(jax.random.fold_in(splits[17], 71), 0)
    ffn_gain = jnp.clip(1.0 + 0.18 * jax.random.normal(splits[12], (D,), jnp.float32), 0.1, 1.9)
    expert_ids_keys = jax.random.split(jax.random.fold_in(splits[13], 1), ROWS // ROW_Q)
    expert_ids_turns = jax.random.permutation(jax.random.fold_in(splits[13], 3), ROWS // ROW_Q)
    expert_ids = jax.vmap(lambda own, number: routed_block(jax.random.fold_in(splits[13], 2), own, number, ROW_Q, EXPERTS, TOPK, MOST, 2))(expert_ids_keys, expert_ids_turns).reshape((ROWS, TOPK))
    route_weights = jnp.clip(jnp.exp(math.log(0.5) - 2.3025851 * jax.random.uniform(splits[14], (ROWS, TOPK), jnp.float32) ** steps_of(splits[14], (ROWS, TOPK), ((0, 8),), -0.2, 0.2)), 0.05, 0.5)
    w_gate_up = gaussian(splits[15], (EXPERTS, 2, FF, D), D ** -0.5, 0.125, ((0, 8), (2, 4)))
    w_down = gaussian(splits[16], (EXPERTS, FF, D), FF ** -0.5, 0.15625, ((0, 8), (1, 4)))
    return dict(hidden=hidden, lengths=lengths, attn_gain=attn_gain, w_query=w_query, w_latent=w_latent, latent_gain=latent_gain, w_rope_key=w_rope_key, w_key_up=w_key_up, w_value_up=w_value_up, w_out=w_out, latent_cache=latent_cache, rope_cache=rope_cache, ffn_gain=ffn_gain, expert_ids=expert_ids, route_weights=route_weights, w_gate_up=w_gate_up, w_down=w_down)


epsilon = 1e-06
far_below = -1e+30

def rms_norm(values, norm_gain):
    mean_square = lax.optimization_barrier(jnp.mean(values * values, axis=-1, keepdims=True))
    return values * lax.rsqrt(mean_square + epsilon) * norm_gain

def rotary(values, positions):
    half_width = values.shape[-1] // 2
    step_index = jnp.arange(half_width, dtype=jnp.float32)
    frequency = jnp.exp(-jnp.log(10000.0) * step_index / half_width)
    angles = positions.astype(jnp.float32)[:, None] * frequency[None, :]
    if values.ndim == 3:
        angles = angles[:, None, :]
    cosine = jnp.cos(angles)
    sine_part = jnp.sin(angles)
    first_half = values[..., :half_width]
    second = values[..., half_width:]
    return jnp.concatenate([first_half * cosine - second * sine_part, second * cosine + first_half * sine_part], axis=-1)

def slot_targets(expert_ids, block_rows):
    row_count, top_count = expert_ids.shape
    blocks = row_count // block_rows
    flat_ids = expert_ids.reshape(blocks, block_rows * top_count)
    onehot = (flat_ids[:, :, None] == jnp.arange(EXPERTS, dtype=jnp.int32)[None, None, :]).astype(jnp.int32)
    earlier = jnp.cumsum(onehot, axis=1) - onehot
    rank_in = lax.optimization_barrier(jnp.sum(earlier * onehot, axis=2))
    capacity = blocks * MOST
    target = flat_ids * capacity + jnp.arange(blocks, dtype=jnp.int32)[:, None] * MOST + rank_in
    return (target.reshape(row_count, top_count).astype(jnp.int32), capacity)

def attend(query_latent, query_rope, latent_new, key_new, latent_cache, rope_cache, lengths, score_scale):
    scores = jnp.einsum('rhl,rtl->rht', query_latent.astype(jnp.float32), latent_cache.astype(jnp.float32))
    scores = scores + jnp.einsum('rhp,rpt->rht', query_rope.astype(jnp.float32), rope_cache.astype(jnp.float32))
    scores = scores * score_scale
    self_score = jnp.einsum('rhl,rl->rh', query_latent.astype(jnp.float32), latent_new.astype(jnp.float32))
    self_score = (self_score + jnp.einsum('rhp,rp->rh', query_rope.astype(jnp.float32), key_new.astype(jnp.float32))) * score_scale
    places = jnp.arange(latent_cache.shape[1], dtype=jnp.int32)
    valid_mask = places[None, None, :] < lengths[:, None, None]
    masked = jnp.where(valid_mask, scores, far_below)
    peak_score = jnp.maximum(lax.optimization_barrier(jnp.max(masked, axis=2)), self_score)
    weights = jnp.where(valid_mask, jnp.exp(masked - peak_score[:, :, None]), 0.0)
    self_weight = jnp.exp(self_score - peak_score)
    totals = lax.optimization_barrier(jnp.sum(weights, axis=2)) + self_weight
    prob_cache = (weights / totals[:, :, None]).astype(jnp.bfloat16)
    prob_self = (self_weight / totals).astype(jnp.bfloat16)
    mixed = jnp.einsum('rht,rtl->rhl', prob_cache.astype(jnp.float32), latent_cache.astype(jnp.float32))
    mixed = mixed + prob_self.astype(jnp.float32)[:, :, None] * latent_new.astype(jnp.float32)[:, None, :]
    return mixed.astype(jnp.bfloat16)

def reference(hidden, lengths, attn_gain, w_query, w_latent, latent_gain, w_rope_key, w_key_up, w_value_up, w_out, latent_cache, rope_cache, ffn_gain, expert_ids, route_weights, w_gate_up, w_down):
    normed = rms_norm(hidden.astype(jnp.float32), attn_gain).astype(jnp.bfloat16)
    queries = jnp.dot(normed, w_query, preferred_element_type=jnp.float32).astype(jnp.bfloat16)
    queries = queries.reshape(ROWS, HEADS, NOPE + ROPE)
    query_rope = rotary(queries[:, :, NOPE:].astype(jnp.float32), lengths).astype(jnp.bfloat16)
    query_latent = jnp.einsum('rhn,hln->rhl', queries[:, :, :NOPE].astype(jnp.float32), w_key_up.astype(jnp.float32)).astype(jnp.bfloat16)
    latent_new = rms_norm(jnp.dot(normed, w_latent, preferred_element_type=jnp.float32), latent_gain).astype(jnp.bfloat16)
    key_raw = lax.dot_general(normed, w_rope_key, (((1,), (1,)), ((), ())), preferred_element_type=jnp.float32)
    key_new = rotary(key_raw, lengths).astype(jnp.bfloat16)
    score_scale = (NOPE + ROPE) ** (-0.5)
    block_count = ROWS // ROW_DEV

    def one_block(pieces):
        q_lat, q_rot, lat_new, k_new, lat_cache, rot_cache, lens = pieces
        mixed_latent = attend(q_lat, q_rot, lat_new, k_new, lat_cache, rot_cache, lens, score_scale)
        head_out = jnp.einsum('rhl,hlv->rhv', mixed_latent.astype(jnp.float32), w_value_up.astype(jnp.float32))
        return head_out.astype(jnp.bfloat16).reshape(ROW_DEV, HEADS * VHEAD)
    head_out = lax.map(one_block, (query_latent.reshape(block_count, ROW_DEV, HEADS, LATENT), query_rope.reshape(block_count, ROW_DEV, HEADS, ROPE), latent_new.reshape(block_count, ROW_DEV, LATENT), key_new.reshape(block_count, ROW_DEV, ROPE), latent_cache.reshape(block_count, ROW_DEV, LEN, LATENT), rope_cache.reshape(block_count, ROW_DEV, ROPE, LEN), lengths.reshape(block_count, ROW_DEV))).reshape(ROWS, HEADS * VHEAD)
    attention = jnp.dot(head_out, w_out, preferred_element_type=jnp.float32)
    middle = (hidden.astype(jnp.float32) + attention).astype(jnp.bfloat16)
    expert_in = rms_norm(middle.astype(jnp.float32), ffn_gain).astype(jnp.bfloat16)
    target, capacity = slot_targets(expert_ids, ROW_Q)
    row_ids = jnp.repeat(jnp.arange(ROWS, dtype=jnp.int32), TOPK)
    row_of = jnp.full((EXPERTS * capacity,), ROWS, jnp.int32).at[target.reshape(-1)].set(row_ids)
    padded = jnp.concatenate([expert_in, jnp.zeros((1, D), jnp.bfloat16)], axis=0)

    def one_expert(pieces):
        picked, gate_up, down_part = pieces
        rows_in = padded[picked]
        gate_part = jnp.dot(rows_in, gate_up[0].T, preferred_element_type=jnp.float32)
        up_part = jnp.dot(rows_in, gate_up[1].T, preferred_element_type=jnp.float32)
        activated = (jax.nn.silu(gate_part) * up_part).astype(jnp.bfloat16)
        return jnp.dot(activated, down_part, preferred_element_type=jnp.float32).astype(jnp.bfloat16)
    outputs = lax.map(one_expert, (row_of.reshape(EXPERTS, capacity), w_gate_up, w_down)).reshape(EXPERTS * capacity, D)
    routed = outputs[target.reshape(-1)].reshape(ROWS, TOPK, D).astype(jnp.float32)
    layer_out = middle.astype(jnp.float32) + lax.optimization_barrier(jnp.sum(route_weights[:, :, None] * routed, axis=1))
    return layer_out.astype(jnp.bfloat16)
```

```python
import functools

import jax
import jax.numpy as jnp
from jax import lax
from jax.experimental import pallas as pl
from jax.experimental.pallas import tpu as pltpu
from jax.sharding import PartitionSpec as P

MOST = 2
CHUNKS = 4
MESH = pl.DeviceIdType.MESH


epsilon = 1e-06
far_below = -1e30


def rms_norm(values, norm_gain):
    mean_square = jnp.mean(values * values, axis=-1, keepdims=True)
    return values * lax.rsqrt(mean_square + epsilon) * norm_gain


def rotary(values, positions):
    half_width = values.shape[-1] // 2
    step_index = jnp.arange(half_width, dtype=jnp.float32)
    frequency = jnp.exp(-jnp.log(10000.0) * step_index / half_width)
    angles = positions.astype(jnp.float32)[:, None] * frequency[None, :]
    if values.ndim == 3:
        angles = angles[:, None, :]
    cosine = jnp.cos(angles)
    sine_part = jnp.sin(angles)
    first_half = values[..., :half_width]
    second = values[..., half_width:]
    return jnp.concatenate(
        [first_half * cosine - second * sine_part, second * cosine + first_half * sine_part],
        axis=-1,
    )


def route_rows(table_ref, ids, weights, experts, place):
    rows, top = ids.shape
    lane = lax.broadcasted_iota(jnp.int32, (rows, experts), 1)
    row = lax.broadcasted_iota(jnp.int32, (rows, experts), 0)
    dense = jnp.zeros((rows, experts), jnp.float32)
    routed = jnp.zeros((rows, experts), jnp.float32)
    for k in range(top):
        hit = lane == ids[:, k : k + 1]
        dense = dense + jnp.where(hit, weights[:, k : k + 1], 0.0)
        routed = routed + jnp.where(hit, 1.0, 0.0)
    rank = jnp.zeros((rows, experts), jnp.float32)
    for j in range(rows - 1):
        rank = rank + jnp.where(row > j, routed[j : j + 1, :], 0.0)
    first = (place * MOST).astype(jnp.float32)
    table_ref[:, :experts] = dense
    table_ref[:, experts:] = jnp.where(routed > 0.0, first + rank, -1.0)


def expert_kernel(
    sections,
    devices,
    part_ref,
    hidden_ref,
    gain_ref,
    ids_ref,
    weights_ref,
    w_up_ref,
    w_down_ref,
    out_ref,
    w_up,
    w_down,
    part_in,
    middle,
    table,
    tables,
    own,
    rows_all,
    pick,
    mix,
    packed,
    lifted,
    activated,
    sum_out,
    pair_in,
    pair_sum,
    plane_in,
    plane_sum,
    line_in,
    own_out,
    finished,
    up_sem,
    down_sem,
    part_send,
    part_recv,
    table_send,
    table_recv,
    line_send,
    line_recv,
    plane_send,
    plane_recv,
    pair_send,
    pair_recv,
    back_pair_send,
    back_pair_recv,
    back_plane_send,
    back_plane_recv,
    back_line_send,
    back_line_recv,
    done_send,
    done_recv,
):
    section = lax.axis_index("section")
    dev = lax.axis_index("dev")
    core = lax.rem(dev, 2)
    line = dev // 2
    pairs = devices // 2
    total = sections * devices
    me = dev * sections + section
    local, _, units, width = w_up.shape
    chunks, quarter, span = own.shape
    rows = total * quarter
    experts = tables.shape[-1] // 2
    slots = packed.shape[0] // local
    bf16, f32 = jnp.bfloat16, jnp.float32
    partner = (section, dev + 1 - 2 * core)

    def remote(source, landing, send, recv, device):
        return pltpu.make_async_remote_copy(
            src_ref=source,
            dst_ref=landing,
            send_sem=send,
            recv_sem=recv,
            device_id=device,
            device_id_type=MESH,
        )

    def up_copy(e):
        return pltpu.make_async_copy(w_up_ref.at[e], w_up.at[e], up_sem.at[e])

    def down_copy(e):
        return pltpu.make_async_copy(w_down_ref.at[e], w_down.at[e], down_sem.at[e])

    @pl.loop(0, local)
    def _(e):
        up_copy(e).start()

    @pl.loop(0, local)
    def _(e):
        down_copy(e).start()

    barrier = pltpu.get_barrier_semaphore()

    @pl.loop(1, total)
    def _(i):
        t = lax.rem(me + i, total)
        pl.semaphore_signal(
            barrier, inc=1, device_id=(lax.rem(t, sections), t // sections), device_id_type=MESH
        )

    pl.semaphore_wait(barrier, total - 1)

    def part_copy(i, here):
        t = lax.rem(section + i, sections)
        return remote(part_ref.at[t], part_in.at[here], part_send.at[i], part_recv.at[here], (t, dev))

    for i in range(1, sections):
        part_copy(i, section).start()

    def place_of(t):
        return (lax.rem(t // sections, 2) * sections + lax.rem(t, sections)) * pairs + t // (
            2 * sections
        )

    here = place_of(me)
    route_rows(table, ids_ref[section], weights_ref[section], experts, here)
    tables[here] = table[...]

    def table_copy(i, landing):
        t = lax.rem(me + i, total)
        return remote(
            table,
            tables.at[landing],
            table_send.at[i],
            table_recv.at[landing],
            (lax.rem(t, sections), t // sections),
        )

    @pl.loop(1, total)
    def _(i):
        table_copy(i, here).start()

    summed = hidden_ref[section].astype(f32) + part_ref[section].astype(f32)
    for i in range(1, sections):
        t = lax.rem(section + i, sections)
        part_copy(i, t).wait_recv()
        summed = summed + part_in[t].astype(f32)
    middle_rows = summed.astype(bf16).astype(f32)
    middle[...] = middle_rows
    normed = rms_norm(middle_rows, gain_ref[...]).astype(bf16)

    def line_copy(k, i, slot):
        t = lax.rem(line + i, pairs)
        return remote(
            own.at[k],
            rows_all.at[k, core, section, slot],
            line_send.at[k, i],
            line_recv.at[k, slot],
            (section, 2 * t + core),
        )

    def plane_copy(k, i, source):
        return remote(
            rows_all.at[k, core, source],
            rows_all.at[k, core, source],
            plane_send.at[k, i],
            plane_recv.at[k, source],
            (lax.rem(section + i, sections), dev),
        )

    def pair_copy(k, which):
        return remote(
            rows_all.at[k, which], rows_all.at[k, which], pair_send.at[k], pair_recv.at[k], partner
        )

    for k in range(chunks):
        own[k] = normed[:, k * span : (k + 1) * span]
        rows_all[k, core, section, line] = normed[:, k * span : (k + 1) * span]

        @pl.loop(1, pairs)
        def _(i):
            line_copy(k, i, line).start()

    for k in range(chunks):

        @pl.loop(1, pairs)
        def _(i):
            line_copy(k, i, lax.rem(line + i, pairs)).wait_recv()

        for i in range(1, sections):
            plane_copy(k, i, section).start()

    @pl.loop(1, total)
    def _(i):
        table_copy(i, place_of(lax.rem(me + i, total))).wait_recv()

    known = tables[...].reshape(rows, 2 * experts).astype(bf16)
    wide = local * slots
    column = lax.broadcasted_iota(jnp.int32, (2 * experts, wide), 1).astype(f32)
    column_expert = jnp.floor((column + 0.5) * (1.0 / slots))
    entry = lax.broadcasted_iota(jnp.int32, (2 * experts, wide), 0)
    entry = (entry - dev * local).astype(f32)
    weight_pick = jnp.where(entry == column_expert, 1.0, 0.0).astype(bf16)
    slot_pick = jnp.where(entry == column_expert + float(experts), 1.0, 0.0).astype(bf16)
    slot_map = jnp.dot(known, slot_pick, preferred_element_type=f32)
    weight_map = jnp.dot(known, weight_pick, preferred_element_type=f32)
    column = lax.broadcasted_iota(jnp.int32, (rows, wide), 1).astype(f32)
    chosen = slot_map == column - jnp.floor((column + 0.5) * (1.0 / slots)) * slots
    pick[...] = jnp.where(chosen, 1.0, 0.0).astype(bf16)
    mix[...] = jnp.where(chosen, weight_map, 0.0).astype(bf16)

    def to_partner(k):
        for i in range(1, sections):
            plane_copy(k, i, lax.rem(section + i, sections)).wait_recv()
        pair_copy(k, core).start()

    flat = (((1,), (1,)), ((), ()))
    to_partner(0)
    for k in range(chunks):
        if k + 1 < chunks:
            to_partner(k + 1)
        pair_copy(k, 1 - core).wait_recv()
        block = rows_all[k].astype(f32).reshape(rows, span).astype(bf16)
        packed[...] = lax.dot_general(
            pick[...], block, (((0,), (0,)), ((), ())), preferred_element_type=f32
        ).astype(bf16)
        for e in range(local):
            if k == 0:
                up_copy(e).wait()
            held = slice(e * slots, (e + 1) * slots)
            both = lax.dot_general(
                packed[held, :],
                w_up[e, :, :, k * span : (k + 1) * span].reshape(2 * units, span),
                flat,
                preferred_element_type=f32,
            )
            if k > 0:
                both = both + lifted[held, :]
            if k + 1 < chunks:
                lifted[held, :] = both
            else:
                gate, lift = both[:, :units], both[:, units:]
                activated[held, :] = (gate / (1.0 + jnp.exp(-gate)) * lift).astype(bf16)

    def back_pair_copy(k, which):
        return remote(
            sum_out.at[k, which], pair_in.at[k], back_pair_send.at[k], back_pair_recv.at[k], partner
        )

    def back_plane_copy(k, i, landing):
        t = lax.rem(section + i, sections)
        return remote(
            pair_sum.at[k, t],
            plane_in.at[k, landing],
            back_plane_send.at[k, i],
            back_plane_recv.at[k, landing],
            (t, dev),
        )

    def back_line_copy(k, i, landing):
        t = lax.rem(line + i, pairs)
        return remote(
            plane_sum.at[k, t],
            line_in.at[k, landing],
            back_line_send.at[k, i],
            back_line_recv.at[k, landing],
            (section, 2 * t + core),
        )

    def done_copy(k, i, landing):
        return remote(
            own_out.at[k],
            finished.at[k, landing],
            done_send.at[k, i],
            done_recv.at[k, landing],
            (lax.rem(section + i, sections), dev),
        )

    def over_plane(k):
        back_pair_copy(k, 1 - core).wait_recv()
        pair_sum[k] = (sum_out[k, core].astype(f32) + pair_in[k].astype(f32)).astype(bf16)
        for i in range(1, sections):
            back_plane_copy(k, i, section).start()

    def over_line(k):
        added = pair_sum[k, section].astype(f32)
        for i in range(1, sections):
            t = lax.rem(section + i, sections)
            back_plane_copy(k, i, t).wait_recv()
            added = added + plane_in[k, t].astype(f32)
        plane_sum[k] = added.astype(bf16)

        @pl.loop(1, pairs)
        def _(i):
            back_line_copy(k, i, line).start()

        line_in[k, line] = plane_sum[k, line]

    def over_sections(k):
        @pl.loop(1, pairs)
        def _(i):
            back_line_copy(k, i, lax.rem(line + i, pairs)).wait_recv()

        result = middle[:, k * span : (k + 1) * span] + jnp.sum(line_in[k].astype(f32), axis=0)
        own_out[k] = result.astype(bf16)
        finished[k, section] = result.astype(bf16)
        for i in range(1, sections):
            done_copy(k, i, section).start()

    for k in range(chunks):
        part_of = slice(k * span, (k + 1) * span)
        outs = []
        for e in range(local):
            if k == 0:
                down_copy(e).wait()
            held = slice(e * slots, (e + 1) * slots)
            outs.append(
                jnp.dot(
                    activated[held, :], w_down[e, :, part_of], preferred_element_type=f32
                ).astype(bf16)
            )
        mixed = jnp.dot(mix[...], jnp.concatenate(outs, axis=0), preferred_element_type=f32)
        sum_out[k] = mixed.reshape(2, sections, pairs, quarter, span).astype(bf16)
        back_pair_copy(k, 1 - core).start()
        if k > 0:
            over_plane(k - 1)
    over_plane(chunks - 1)
    for k in range(chunks):
        over_line(k)
    for k in range(chunks):
        over_sections(k)
    for k in range(chunks):
        for i in range(1, sections):
            done_copy(k, i, lax.rem(section + i, sections)).wait_recv()
        out_ref[:, :, k * span : (k + 1) * span] = finished[k]

    for i in range(1, sections):
        part_copy(i, section).wait_send()

    @pl.loop(1, total)
    def _(i):
        table_copy(i, here).wait_send()

    for k in range(chunks):

        @pl.loop(1, pairs)
        def _(i):
            line_copy(k, i, line).wait_send()
            back_line_copy(k, i, line).wait_send()

        for i in range(1, sections):
            plane_copy(k, i, section).wait_send()
            back_plane_copy(k, i, section).wait_send()
            done_copy(k, i, section).wait_send()
        pair_copy(k, core).wait_send()
        back_pair_copy(k, 1 - core).wait_send()


def expert_layer(part, hidden, ffn_gain, expert_ids, route_weights, w_gate_up, w_down):
    sections = lax.axis_size("section")
    devices = lax.axis_size("dev")
    total = sections * devices
    pairs = devices // 2
    row_count, width = hidden.shape
    quarter = row_count // sections
    local, _, units, _ = w_gate_up.shape
    experts = local * devices
    slots = total * MOST
    rows = total * quarter
    chunks = CHUNKS
    span = width // chunks
    bf16, f32 = jnp.bfloat16, jnp.float32
    vmem = pl.BlockSpec(memory_space=pltpu.VMEM)
    anywhere = pl.BlockSpec(memory_space=pl.ANY)
    sems = lambda *count: pltpu.SemaphoreType.DMA(count)
    out = pl.pallas_call(
        functools.partial(expert_kernel, sections, devices),
        out_shape=jax.ShapeDtypeStruct((sections, quarter, width), bf16),
        in_specs=[vmem] * 5 + [anywhere] * 2,
        out_specs=vmem,
        scratch_shapes=[
            pltpu.VMEM(w_gate_up.shape, bf16),
            pltpu.VMEM(w_down.shape, bf16),
            pltpu.VMEM((sections, quarter, width), bf16),
            pltpu.VMEM((quarter, width), f32),
            pltpu.VMEM((quarter, 2 * experts), f32),
            pltpu.VMEM((total, quarter, 2 * experts), f32),
            pltpu.VMEM((chunks, quarter, span), bf16),
            pltpu.VMEM((chunks, 2, sections, pairs, quarter, span), bf16),
            pltpu.VMEM((rows, local * slots), bf16),
            pltpu.VMEM((rows, local * slots), bf16),
            pltpu.VMEM((local * slots, span), bf16),
            pltpu.VMEM((local * slots, 2 * units), f32),
            pltpu.VMEM((local * slots, units), bf16),
            pltpu.VMEM((chunks, 2, sections, pairs, quarter, span), bf16),
            pltpu.VMEM((chunks, sections, pairs, quarter, span), bf16),
            pltpu.VMEM((chunks, sections, pairs, quarter, span), bf16),
            pltpu.VMEM((chunks, sections, pairs, quarter, span), bf16),
            pltpu.VMEM((chunks, pairs, quarter, span), bf16),
            pltpu.VMEM((chunks, pairs, quarter, span), bf16),
            pltpu.VMEM((chunks, quarter, span), bf16),
            pltpu.VMEM((chunks, sections, quarter, span), bf16),
            sems(local),
            sems(local),
            sems(sections),
            sems(sections),
            sems(total),
            sems(total),
            sems(chunks, pairs),
            sems(chunks, pairs),
            sems(chunks, sections),
            sems(chunks, sections),
            sems(chunks),
            sems(chunks),
            sems(chunks),
            sems(chunks),
            sems(chunks, sections),
            sems(chunks, sections),
            sems(chunks, pairs),
            sems(chunks, pairs),
            sems(chunks, sections),
            sems(chunks, sections),
        ],
        compiler_params=pltpu.CompilerParams(
            collective_id=0, has_side_effects=True, vmem_limit_bytes=62 * 1024 * 1024
        ),
    )(
        part.astype(bf16).reshape(sections, quarter, width),
        hidden.reshape(sections, quarter, width),
        ffn_gain.reshape(1, width),
        expert_ids.reshape(sections, quarter, -1),
        route_weights.reshape(sections, quarter, -1),
        w_gate_up,
        w_down,
    )
    return out.reshape(row_count, width)


def attend(
    query_latent, query_rope, latent_new, key_new, latent_cache, rope_cache, lengths, score_scale
):
    scores = jnp.einsum(
        "rhl,rtl->rht", query_latent, latent_cache, preferred_element_type=jnp.float32
    )
    scores = scores + jnp.einsum(
        "rhp,rpt->rht", query_rope, rope_cache, preferred_element_type=jnp.float32
    )
    scores = scores * score_scale
    self_score = jnp.einsum(
        "rhl,rl->rh", query_latent, latent_new, preferred_element_type=jnp.float32
    )
    self_score = (
        self_score
        + jnp.einsum("rhp,rp->rh", query_rope, key_new, preferred_element_type=jnp.float32)
    ) * score_scale
    places = jnp.arange(latent_cache.shape[1], dtype=jnp.int32)
    valid_mask = places[None, None, :] < lengths[:, None, None]
    masked = jnp.where(valid_mask, scores, far_below)
    peak_score = jnp.maximum(jnp.max(masked, axis=2), self_score)
    weights = jnp.where(valid_mask, jnp.exp(masked - peak_score[:, :, None]), 0.0)
    self_weight = jnp.exp(self_score - peak_score)
    totals = jnp.sum(weights, axis=2) + self_weight
    prob_cache = (weights / totals[:, :, None]).astype(jnp.bfloat16)
    prob_self = (self_weight / totals).astype(jnp.bfloat16)
    mixed = jnp.einsum("rht,rtl->rhl", prob_cache, latent_cache, preferred_element_type=jnp.float32)
    mixed = (
        mixed
        + prob_self.astype(jnp.float32)[:, :, None] * latent_new.astype(jnp.float32)[:, None, :]
    )
    return mixed.astype(jnp.bfloat16)


def per_device(
    hidden,
    lengths,
    attn_gain,
    w_query,
    w_latent,
    latent_gain,
    w_rope_key,
    w_key_up,
    w_value_up,
    w_out,
    latent_cache,
    rope_cache,
    ffn_gain,
    expert_ids,
    route_weights,
    w_gate_up,
    w_down,
):
    row_count = hidden.shape[0]
    head_local = w_key_up.shape[0]
    nope_width = w_key_up.shape[2]
    rope_width = w_rope_key.shape[0]
    score_scale = (nope_width + rope_width) ** (-0.5)
    normed = rms_norm(hidden.astype(jnp.float32), attn_gain).astype(jnp.bfloat16)
    queries = jnp.dot(normed, w_query, preferred_element_type=jnp.float32).astype(jnp.bfloat16)
    queries = queries.reshape(row_count, head_local, nope_width + rope_width)
    query_rope = rotary(queries[:, :, nope_width:].astype(jnp.float32), lengths).astype(
        jnp.bfloat16
    )
    query_latent = jnp.einsum(
        "rhn,hln->rhl", queries[:, :, :nope_width], w_key_up, preferred_element_type=jnp.float32
    ).astype(jnp.bfloat16)
    latent_new = rms_norm(
        jnp.dot(normed, w_latent, preferred_element_type=jnp.float32), latent_gain
    ).astype(jnp.bfloat16)
    key_raw = lax.dot_general(
        normed, w_rope_key, (((1,), (1,)), ((), ())), preferred_element_type=jnp.float32
    )
    key_new = rotary(key_raw, lengths).astype(jnp.bfloat16)
    mixed_latent = attend(
        query_latent,
        query_rope,
        latent_new,
        key_new,
        latent_cache,
        rope_cache,
        lengths,
        score_scale,
    )
    head_out = jnp.einsum(
        "rhl,hlv->rhv", mixed_latent, w_value_up, preferred_element_type=jnp.float32
    ).astype(jnp.bfloat16)
    heads_flat = head_out.reshape(row_count, -1)
    part = jnp.dot(heads_flat, w_out, preferred_element_type=jnp.float32)
    return expert_layer(part, hidden, ffn_gain, expert_ids, route_weights, w_gate_up, w_down)


def solution(mesh):
    in_specs = (
        P("dev", None),
        P("dev"),
        P(),
        P(None, "section"),
        P(),
        P(),
        P(),
        P("section", None, None),
        P("section", None, None),
        P("section", None),
        P("dev", None, None),
        P("dev", None, None),
        P(),
        P("dev", None),
        P("dev", None),
        P("dev", None, "section", None),
        P("dev", "section", None),
    )
    out_specs = P("dev", None)
    return jax.shard_map(
        per_device, mesh=mesh, in_specs=in_specs, out_specs=out_specs, check_vma=False
    )
```

```python
import functools

import jax
import jax.numpy as jnp
from jax import lax
from jax.experimental import pallas as pl
from jax.experimental.pallas import tpu as pltpu
from jax.sharding import PartitionSpec as P

MOST = 2
CHUNKS = 4
CACHE_GROUPS = 8
MESH = pl.DeviceIdType.MESH


epsilon = 1e-06
far_below = -1e30


def rms_norm(values, norm_gain):
    mean_square = jnp.mean(values * values, axis=-1, keepdims=True)
    return values * lax.rsqrt(mean_square + epsilon) * norm_gain


def turn_of(positions, width):
    half = width // 2
    step = lax.broadcasted_iota(jnp.int32, (1, width), 1)
    step = jnp.where(step < half, step, step - half).astype(jnp.float32)
    frequency = jnp.exp(-jnp.log(10000.0) * step / half)
    angles = positions.astype(jnp.float32) * frequency
    return jnp.cos(angles), jnp.sin(angles)


def rotary(values, cosine, sine):
    half = values.shape[-1] // 2
    turned = jnp.concatenate([-values[:, half:], values[:, :half]], axis=1)
    return values * cosine + turned * sine


def route_rows(table_ref, ids_ref, weights_ref, first_row, experts, place):
    rows = table_ref.shape[0]
    lane = lax.broadcasted_iota(jnp.int32, (rows, experts), 1)
    row = lax.broadcasted_iota(jnp.int32, (rows, experts), 0)
    dense = jnp.zeros((rows, experts), jnp.float32)
    routed = jnp.zeros((rows, experts), jnp.float32)
    for i in range(rows):
        for k in range(ids_ref.shape[0]):
            hit = (row == i) & (lane == ids_ref[k, first_row + i])
            dense = jnp.where(hit, weights_ref[k, first_row + i], dense)
            routed = jnp.where(hit, 1.0, routed)
    rank = jnp.zeros((rows, experts), jnp.float32)
    for j in range(rows - 1):
        rank = rank + jnp.where(row > j, routed[j : j + 1, :], 0.0)
    first = (place * MOST).astype(jnp.float32)
    table_ref[:, :experts] = dense
    table_ref[:, experts:] = jnp.where(routed > 0.0, first + rank, -1.0)


def layer_kernel(
    sections,
    devices,
    lengths_ref,
    ids_ref,
    weights_ref,
    hidden_ref,
    attn_gain_ref,
    latent_gain_ref,
    ffn_gain_ref,
    w_query_ref,
    w_latent_ref,
    w_rope_key_ref,
    w_key_up_ref,
    w_value_up_ref,
    w_out_ref,
    latent_cache_ref,
    rope_cache_ref,
    w_up_ref,
    w_down_ref,
    out_ref,
    hidden_in,
    attn_gain,
    latent_gain,
    ffn_gain,
    w_query,
    w_latent,
    w_rope_key,
    w_key_up,
    w_value_up,
    w_out,
    latents,
    ropes,
    residual,
    query_latent,
    query_rope,
    self_scores,
    scores,
    mixed_latent,
    part_out,
    w_up,
    w_down,
    part_in,
    middle,
    table,
    tables,
    own,
    rows_all,
    pick,
    mix,
    packed,
    lifted,
    activated,
    sum_out,
    pair_in,
    pair_sum,
    plane_in,
    plane_sum,
    line_in,
    own_out,
    finished,
    early_sem,
    cache_sem,
    up_sem,
    down_sem,
    part_send,
    part_recv,
    table_send,
    table_recv,
    line_send,
    line_recv,
    plane_send,
    plane_recv,
    pair_send,
    pair_recv,
    back_pair_send,
    back_pair_recv,
    back_plane_send,
    back_plane_recv,
    back_line_send,
    back_line_recv,
    done_send,
    done_recv,
):
    section = lax.axis_index("section")
    dev = lax.axis_index("dev")
    core = lax.rem(dev, 2)
    line = dev // 2
    pairs = devices // 2
    total = sections * devices
    me = dev * sections + section
    local, _, units, width = w_up.shape
    chunks, quarter, span = own.shape
    rows = total * quarter
    experts = tables.shape[-1] // 2
    slots = packed.shape[0] // local
    bf16, f32 = jnp.bfloat16, jnp.float32
    partner = (section, dev + 1 - 2 * core)

    def remote(source, landing, send, recv, device):
        return pltpu.make_async_remote_copy(
            src_ref=source,
            dst_ref=landing,
            send_sem=send,
            recv_sem=recv,
            device_id=device,
            device_id_type=MESH,
        )

    def up_copy(e):
        return pltpu.make_async_copy(w_up_ref.at[e], w_up.at[e], up_sem.at[e])

    def down_copy(e):
        return pltpu.make_async_copy(w_down_ref.at[e], w_down.at[e], down_sem.at[e])

    heads, latent, nope = w_key_up.shape
    row_count, slots_kept, _ = latents.shape
    rope = w_rope_key.shape[0]
    padded = scores.shape[0] // row_count
    groups = cache_sem.shape[0] // 2
    group = row_count // groups
    score_scale = (nope + rope) ** (-0.5)
    flat = (((1,), (1,)), ((), ()))

    def early_copy(source, landing, n):
        return pltpu.make_async_copy(source, landing, early_sem.at[n])

    query_copy = early_copy(w_query_ref, w_query, 0)
    key_up_copy = early_copy(w_key_up_ref, w_key_up, 1)
    latent_copy = early_copy(w_latent_ref, w_latent, 2)
    rope_key_copy = early_copy(w_rope_key_ref, w_rope_key, 3)
    value_up_copy = early_copy(w_value_up_ref, w_value_up, 4)
    out_copy = early_copy(w_out_ref, w_out, 5)

    def cache_copies(g):
        held = pl.ds(g * group, group)
        return (
            pltpu.make_async_copy(latent_cache_ref.at[held], latents.at[held], cache_sem.at[2 * g]),
            pltpu.make_async_copy(rope_cache_ref.at[held], ropes.at[held], cache_sem.at[2 * g + 1]),
        )

    hidden_copy = early_copy(hidden_ref, hidden_in, 6)
    gain_copies = (
        early_copy(attn_gain_ref, attn_gain, 7),
        early_copy(latent_gain_ref, latent_gain, 8),
        early_copy(ffn_gain_ref, ffn_gain, 9),
    )

    hidden_copy.start()
    for copy in gain_copies:
        copy.start()
    query_copy.start()
    key_up_copy.start()
    latent_copy.start()
    rope_key_copy.start()
    for g in range(groups):
        for copy in cache_copies(g):
            copy.start()
    value_up_copy.start()
    out_copy.start()

    barrier = pltpu.get_barrier_semaphore()

    @pl.loop(1, total)
    def _(i):
        t = lax.rem(me + i, total)
        pl.semaphore_signal(
            barrier, inc=1, device_id=(lax.rem(t, sections), t // sections), device_id_type=MESH
        )

    row = lax.broadcasted_iota(jnp.int32, (row_count, rope), 0)
    positions = jnp.zeros((row_count, rope), jnp.int32)
    for r in range(row_count):
        positions = jnp.where(row == r, lengths_ref[r], positions)
    cosine, sine = turn_of(positions, rope)
    hidden_copy.wait()
    for copy in gain_copies:
        copy.wait()
    hidden = hidden_in[...].astype(f32)
    residual[...] = hidden
    normed = rms_norm(hidden, attn_gain[...]).astype(bf16)
    query_latent[...] = jnp.zeros_like(query_latent)
    query_rope[...] = jnp.zeros_like(query_rope)
    query_copy.wait()
    queries = jnp.dot(normed, w_query[...], preferred_element_type=f32).astype(bf16).astype(f32)
    rope_key_copy.wait()
    latent_copy.wait()
    key_raw = lax.dot_general(normed, w_rope_key[...], flat, preferred_element_type=f32)
    key_new = rotary(key_raw, cosine, sine).astype(bf16).astype(f32)
    latent_raw = jnp.dot(normed, w_latent[...], preferred_element_type=f32)
    latent_new = rms_norm(latent_raw, latent_gain[...]).astype(bf16).astype(f32)
    key_up_copy.wait()
    for h in range(heads):
        first = h * (nope + rope)
        turned = rotary(queries[:, first + nope : first + nope + rope], cosine, sine)
        turned = turned.astype(bf16).astype(f32)
        mapped = lax.dot_general(
            queries[:, first : first + nope].astype(bf16),
            w_key_up[h],
            flat,
            preferred_element_type=f32,
        )
        mapped = mapped.astype(bf16).astype(f32)
        query_latent[:, h, :] = mapped
        query_rope[:, h, :] = turned
        own_score = jnp.sum(mapped * latent_new, axis=1, keepdims=True) + jnp.sum(
            turned * key_new, axis=1, keepdims=True
        )
        self_scores[:, h, :] = jnp.broadcast_to(own_score * score_scale, (row_count, 128))

    place = lax.broadcasted_iota(jnp.int32, (padded, slots_kept), 1)
    for g in range(groups):
        for copy in cache_copies(g):
            copy.wait()
        for e in range(g * local // groups, (g + 1) * local // groups):
            up_copy(e).start()
        for r in range(g * group, (g + 1) * group):
            found = lax.dot_general(
                query_latent[r].astype(bf16), latents[r], flat, preferred_element_type=f32
            ) + jnp.dot(query_rope[r].astype(bf16), ropes[r], preferred_element_type=f32)
            scores[r * padded : (r + 1) * padded, :] = jnp.where(
                place < lengths_ref[r], found * score_scale, far_below
            )
    for e in range(local):
        down_copy(e).start()

    own_scores = self_scores[...].reshape(row_count * padded, 128)[:, :1]
    peak = jnp.maximum(jnp.max(scores[...], axis=1, keepdims=True), own_scores)
    likely = jnp.exp(scores[...] - peak)
    own_likely = jnp.exp(own_scores - peak)
    totals = jnp.sum(likely, axis=1, keepdims=True) + own_likely
    scores[...] = likely / totals
    own_probs = (own_likely / totals).astype(bf16).astype(f32)
    self_scores[...] = jnp.broadcast_to(own_probs, (row_count * padded, 128)).reshape(
        row_count, padded, 128
    )

    for r in range(row_count):
        mixed_latent[r] = jnp.dot(
            scores[r * padded : (r + 1) * padded, :].astype(bf16),
            latents[r],
            preferred_element_type=f32,
        )
    value_up_copy.wait()
    head_outs = []
    for h in range(heads):
        mixed = mixed_latent[:, h, :] + self_scores[:, h, :1] * latent_new
        head_outs.append(
            jnp.dot(mixed.astype(bf16), w_value_up[h], preferred_element_type=f32).astype(bf16)
        )
    out_copy.wait()
    part = jnp.dot(jnp.concatenate(head_outs, axis=1), w_out[...], preferred_element_type=f32)
    for t in range(sections):
        part_out[t] = part[t * quarter : (t + 1) * quarter, :].astype(bf16)

    pl.semaphore_wait(barrier, total - 1)

    def part_copy(i, here):
        t = lax.rem(section + i, sections)
        return remote(part_out.at[t], part_in.at[here], part_send.at[i], part_recv.at[here], (t, dev))

    for i in range(1, sections):
        part_copy(i, section).start()

    def place_of(t):
        return (lax.rem(t // sections, 2) * sections + lax.rem(t, sections)) * pairs + t // (
            2 * sections
        )

    here = place_of(me)
    route_rows(table, ids_ref, weights_ref, section * quarter, experts, here)
    tables[here] = table[...]

    def table_copy(i, landing):
        t = lax.rem(me + i, total)
        return remote(
            table,
            tables.at[landing],
            table_send.at[i],
            table_recv.at[landing],
            (lax.rem(t, sections), t // sections),
        )

    @pl.loop(1, total)
    def _(i):
        table_copy(i, here).start()

    mine = pl.ds(pl.multiple_of(section * quarter, quarter), quarter)
    summed = residual[mine, :] + part_out[section].astype(f32)
    for i in range(1, sections):
        t = lax.rem(section + i, sections)
        part_copy(i, t).wait_recv()
        summed = summed + part_in[t].astype(f32)
    middle_rows = summed.astype(bf16).astype(f32)
    middle[...] = middle_rows
    normed = rms_norm(middle_rows, ffn_gain[...]).astype(bf16)

    def line_copy(k, i, slot):
        t = lax.rem(line + i, pairs)
        return remote(
            own.at[k],
            rows_all.at[k, core, section, slot],
            line_send.at[k, i],
            line_recv.at[k, slot],
            (section, 2 * t + core),
        )

    def plane_copy(k, i, source):
        return remote(
            rows_all.at[k, core, source],
            rows_all.at[k, core, source],
            plane_send.at[k, i],
            plane_recv.at[k, source],
            (lax.rem(section + i, sections), dev),
        )

    def pair_copy(k, which):
        return remote(
            rows_all.at[k, which], rows_all.at[k, which], pair_send.at[k], pair_recv.at[k], partner
        )

    for k in range(chunks):
        own[k] = normed[:, k * span : (k + 1) * span]
        rows_all[k, core, section, line] = normed[:, k * span : (k + 1) * span]

        @pl.loop(1, pairs)
        def _(i):
            line_copy(k, i, line).start()

    for k in range(chunks):

        @pl.loop(1, pairs)
        def _(i):
            line_copy(k, i, lax.rem(line + i, pairs)).wait_recv()

        for i in range(1, sections):
            plane_copy(k, i, section).start()

    @pl.loop(1, total)
    def _(i):
        table_copy(i, place_of(lax.rem(me + i, total))).wait_recv()

    known = tables[...].reshape(rows, 2 * experts).astype(bf16)
    wide = local * slots
    column = lax.broadcasted_iota(jnp.int32, (2 * experts, wide), 1).astype(f32)
    column_expert = jnp.floor((column + 0.5) * (1.0 / slots))
    entry = lax.broadcasted_iota(jnp.int32, (2 * experts, wide), 0)
    entry = (entry - dev * local).astype(f32)
    weight_pick = jnp.where(entry == column_expert, 1.0, 0.0).astype(bf16)
    slot_pick = jnp.where(entry == column_expert + float(experts), 1.0, 0.0).astype(bf16)
    slot_map = jnp.dot(known, slot_pick, preferred_element_type=f32)
    weight_map = jnp.dot(known, weight_pick, preferred_element_type=f32)
    column = lax.broadcasted_iota(jnp.int32, (rows, wide), 1).astype(f32)
    chosen = slot_map == column - jnp.floor((column + 0.5) * (1.0 / slots)) * slots
    pick[...] = jnp.where(chosen, 1.0, 0.0).astype(bf16)
    mix[...] = jnp.where(chosen, weight_map, 0.0).astype(bf16)

    def to_partner(k):
        for i in range(1, sections):
            plane_copy(k, i, lax.rem(section + i, sections)).wait_recv()
        pair_copy(k, core).start()

    to_partner(0)
    for k in range(chunks):
        if k + 1 < chunks:
            to_partner(k + 1)
        pair_copy(k, 1 - core).wait_recv()
        block = rows_all[k].astype(f32).reshape(rows, span).astype(bf16)
        packed[...] = lax.dot_general(
            pick[...], block, (((0,), (0,)), ((), ())), preferred_element_type=f32
        ).astype(bf16)
        for e in range(local):
            if k == 0:
                up_copy(e).wait()
            held = slice(e * slots, (e + 1) * slots)
            both = lax.dot_general(
                packed[held, :],
                w_up[e, :, :, k * span : (k + 1) * span].reshape(2 * units, span),
                flat,
                preferred_element_type=f32,
            )
            if k > 0:
                both = both + lifted[held, :]
            if k + 1 < chunks:
                lifted[held, :] = both
            else:
                gate, lift = both[:, :units], both[:, units:]
                activated[held, :] = (gate / (1.0 + jnp.exp(-gate)) * lift).astype(bf16)

    def back_pair_copy(k, which):
        return remote(
            sum_out.at[k, which], pair_in.at[k], back_pair_send.at[k], back_pair_recv.at[k], partner
        )

    def back_plane_copy(k, i, landing):
        t = lax.rem(section + i, sections)
        return remote(
            pair_sum.at[k, t],
            plane_in.at[k, landing],
            back_plane_send.at[k, i],
            back_plane_recv.at[k, landing],
            (t, dev),
        )

    def back_line_copy(k, i, landing):
        t = lax.rem(line + i, pairs)
        return remote(
            plane_sum.at[k, t],
            line_in.at[k, landing],
            back_line_send.at[k, i],
            back_line_recv.at[k, landing],
            (section, 2 * t + core),
        )

    def done_copy(k, i, landing):
        return remote(
            own_out.at[k],
            finished.at[k, landing],
            done_send.at[k, i],
            done_recv.at[k, landing],
            (lax.rem(section + i, sections), dev),
        )

    def over_plane(k):
        back_pair_copy(k, 1 - core).wait_recv()
        pair_sum[k] = (sum_out[k, core].astype(f32) + pair_in[k].astype(f32)).astype(bf16)
        for i in range(1, sections):
            back_plane_copy(k, i, section).start()

    def over_line(k):
        added = pair_sum[k, section].astype(f32)
        for i in range(1, sections):
            t = lax.rem(section + i, sections)
            back_plane_copy(k, i, t).wait_recv()
            added = added + plane_in[k, t].astype(f32)
        plane_sum[k] = added.astype(bf16)

        @pl.loop(1, pairs)
        def _(i):
            back_line_copy(k, i, line).start()

        line_in[k, line] = plane_sum[k, line]

    def over_sections(k):
        @pl.loop(1, pairs)
        def _(i):
            back_line_copy(k, i, lax.rem(line + i, pairs)).wait_recv()

        result = middle[:, k * span : (k + 1) * span] + jnp.sum(line_in[k].astype(f32), axis=0)
        own_out[k] = result.astype(bf16)
        finished[k, section] = result.astype(bf16)
        for i in range(1, sections):
            done_copy(k, i, section).start()

    for k in range(chunks):
        part_of = slice(k * span, (k + 1) * span)
        outs = []
        for e in range(local):
            if k == 0:
                down_copy(e).wait()
            held = slice(e * slots, (e + 1) * slots)
            outs.append(
                jnp.dot(
                    activated[held, :], w_down[e, :, part_of], preferred_element_type=f32
                ).astype(bf16)
            )
        mixed = jnp.dot(mix[...], jnp.concatenate(outs, axis=0), preferred_element_type=f32)
        sum_out[k] = mixed.reshape(2, sections, pairs, quarter, span).astype(bf16)
        back_pair_copy(k, 1 - core).start()
        if k > 0:
            over_plane(k - 1)
    over_plane(chunks - 1)
    for k in range(chunks):
        over_line(k)
    for k in range(chunks):
        over_sections(k)
    for k in range(chunks):
        for i in range(1, sections):
            done_copy(k, i, lax.rem(section + i, sections)).wait_recv()
        out_ref[:, :, k * span : (k + 1) * span] = finished[k]

    for i in range(1, sections):
        part_copy(i, section).wait_send()

    @pl.loop(1, total)
    def _(i):
        table_copy(i, here).wait_send()

    for k in range(chunks):

        @pl.loop(1, pairs)
        def _(i):
            line_copy(k, i, line).wait_send()
            back_line_copy(k, i, line).wait_send()

        for i in range(1, sections):
            plane_copy(k, i, section).wait_send()
            back_plane_copy(k, i, section).wait_send()
            done_copy(k, i, section).wait_send()
        pair_copy(k, core).wait_send()
        back_pair_copy(k, 1 - core).wait_send()


def per_device(
    hidden,
    lengths,
    attn_gain,
    w_query,
    w_latent,
    latent_gain,
    w_rope_key,
    w_key_up,
    w_value_up,
    w_out,
    latent_cache,
    rope_cache,
    ffn_gain,
    expert_ids,
    route_weights,
    w_gate_up,
    w_down,
):
    sections = lax.axis_size("section")
    devices = lax.axis_size("dev")
    total = sections * devices
    pairs = devices // 2
    row_count, width = hidden.shape
    quarter = row_count // sections
    heads, latent, _ = w_key_up.shape
    rope, slots_kept = rope_cache.shape[1:]
    local, _, units, _ = w_gate_up.shape
    experts = local * devices
    slots = total * MOST
    rows = total * quarter
    chunks = CHUNKS
    span = width // chunks
    groups = CACHE_GROUPS
    padded = -(-heads // 8) * 8
    bf16, f32 = jnp.bfloat16, jnp.float32
    vmem = pl.BlockSpec(memory_space=pltpu.VMEM)
    smem = pl.BlockSpec(memory_space=pltpu.SMEM)
    anywhere = pl.BlockSpec(memory_space=pl.ANY)
    sems = lambda *count: pltpu.SemaphoreType.DMA(count)
    out = pl.pallas_call(
        functools.partial(layer_kernel, sections, devices),
        out_shape=jax.ShapeDtypeStruct((sections, quarter, width), bf16),
        in_specs=[smem] * 3 + [anywhere] * 14,
        out_specs=vmem,
        scratch_shapes=[
            pltpu.VMEM(hidden.shape, bf16),
            pltpu.VMEM((1, width), f32),
            pltpu.VMEM((1, latent), f32),
            pltpu.VMEM((1, width), f32),
            pltpu.VMEM(w_query.shape, bf16),
            pltpu.VMEM(w_latent.shape, bf16),
            pltpu.VMEM(w_rope_key.shape, bf16),
            pltpu.VMEM(w_key_up.shape, bf16),
            pltpu.VMEM(w_value_up.shape, bf16),
            pltpu.VMEM(w_out.shape, bf16),
            pltpu.VMEM(latent_cache.shape, bf16),
            pltpu.VMEM(rope_cache.shape, bf16),
            pltpu.VMEM((row_count, width), f32),
            pltpu.VMEM((row_count, padded, latent), f32),
            pltpu.VMEM((row_count, padded, rope), f32),
            pltpu.VMEM((row_count, padded, 128), f32),
            pltpu.VMEM((row_count * padded, slots_kept), f32),
            pltpu.VMEM((row_count, padded, latent), f32),
            pltpu.VMEM((sections, quarter, width), bf16),
            pltpu.VMEM(w_gate_up.shape, bf16),
            pltpu.VMEM(w_down.shape, bf16),
            pltpu.VMEM((sections, quarter, width), bf16),
            pltpu.VMEM((quarter, width), f32),
            pltpu.VMEM((quarter, 2 * experts), f32),
            pltpu.VMEM((total, quarter, 2 * experts), f32),
            pltpu.VMEM((chunks, quarter, span), bf16),
            pltpu.VMEM((chunks, 2, sections, pairs, quarter, span), bf16),
            pltpu.VMEM((rows, local * slots), bf16),
            pltpu.VMEM((rows, local * slots), bf16),
            pltpu.VMEM((local * slots, span), bf16),
            pltpu.VMEM((local * slots, 2 * units), f32),
            pltpu.VMEM((local * slots, units), bf16),
            pltpu.VMEM((chunks, 2, sections, pairs, quarter, span), bf16),
            pltpu.VMEM((chunks, sections, pairs, quarter, span), bf16),
            pltpu.VMEM((chunks, sections, pairs, quarter, span), bf16),
            pltpu.VMEM((chunks, sections, pairs, quarter, span), bf16),
            pltpu.VMEM((chunks, pairs, quarter, span), bf16),
            pltpu.VMEM((chunks, pairs, quarter, span), bf16),
            pltpu.VMEM((chunks, quarter, span), bf16),
            pltpu.VMEM((chunks, sections, quarter, span), bf16),
            sems(10),
            sems(2 * groups),
            sems(local),
            sems(local),
            sems(sections),
            sems(sections),
            sems(total),
            sems(total),
            sems(chunks, pairs),
            sems(chunks, pairs),
            sems(chunks, sections),
            sems(chunks, sections),
            sems(chunks),
            sems(chunks),
            sems(chunks),
            sems(chunks),
            sems(chunks, sections),
            sems(chunks, sections),
            sems(chunks, pairs),
            sems(chunks, pairs),
            sems(chunks, sections),
            sems(chunks, sections),
        ],
        compiler_params=pltpu.CompilerParams(
            collective_id=0, has_side_effects=True, vmem_limit_bytes=63 * 1024 * 1024
        ),
    )(
        lengths,
        expert_ids.T,
        route_weights.T,
        hidden,
        attn_gain.reshape(1, width),
        latent_gain.reshape(1, latent),
        ffn_gain.reshape(1, width),
        w_query,
        w_latent,
        w_rope_key,
        w_key_up,
        w_value_up,
        w_out,
        latent_cache,
        rope_cache,
        w_gate_up,
        w_down,
    )
    return out.reshape(row_count, width)


def solution(mesh):
    in_specs = (
        P("dev", None),
        P("dev"),
        P(),
        P(None, "section"),
        P(),
        P(),
        P(),
        P("section", None, None),
        P("section", None, None),
        P("section", None),
        P("dev", None, None),
        P("dev", None, None),
        P(),
        P("dev", None),
        P("dev", None),
        P("dev", None, "section", None),
        P("dev", "section", None),
    )
    out_specs = P("dev", None)
    return jax.shard_map(
        per_device, mesh=mesh, in_specs=in_specs, out_specs=out_specs, check_vma=False
    )
```

```python
import functools

import jax
import jax.numpy as jnp
from jax import lax
from jax.experimental import pallas as pl
from jax.experimental.pallas import tpu as pltpu
from jax.sharding import PartitionSpec as P

MOST = 2
OUT_CHUNKS = 4
BACK_CHUNKS = 4
CACHE_GROUPS = 4
MESH = pl.DeviceIdType.MESH


epsilon = 1e-06
far_below = -1e30


def rms_norm(values, norm_gain):
    mean_square = jnp.mean(values * values, axis=-1, keepdims=True)
    return values * lax.rsqrt(mean_square + epsilon) * norm_gain


def turn_of(positions, width):
    half = width // 2
    step = lax.broadcasted_iota(jnp.int32, (1, width), 1)
    step = jnp.where(step < half, step, step - half).astype(jnp.float32)
    frequency = jnp.exp(-jnp.log(10000.0) * step / half)
    angles = positions.astype(jnp.float32) * frequency
    return jnp.cos(angles), jnp.sin(angles)


def rotary(values, cosine, sine):
    half = values.shape[-1] // 2
    turned = jnp.concatenate([-values[:, half:], values[:, :half]], axis=1)
    return values * cosine + turned * sine


def route_rows(table_ref, ids_ref, weights_ref, first_row, experts, place):
    rows = table_ref.shape[0]
    lane = lax.broadcasted_iota(jnp.int32, (rows, experts), 1)
    row = lax.broadcasted_iota(jnp.int32, (rows, experts), 0)
    dense = jnp.zeros((rows, experts), jnp.float32)
    routed = jnp.zeros((rows, experts), jnp.float32)
    for i in range(rows):
        for k in range(ids_ref.shape[0]):
            hit = (row == i) & (lane == ids_ref[k, first_row + i])
            dense = jnp.where(hit, weights_ref[k, first_row + i], dense)
            routed = jnp.where(hit, 1.0, routed)
    rank = jnp.zeros((rows, experts), jnp.float32)
    for j in range(rows - 1):
        rank = rank + jnp.where(row > j, routed[j : j + 1, :], 0.0)
    first = (place * MOST).astype(jnp.float32)
    table_ref[:, :experts] = dense
    table_ref[:, experts:] = jnp.where(routed > 0.0, first + rank, -1.0)


def layer_kernel(
    sections,
    devices,
    lengths_in,
    ids_in,
    weights_in,
    hidden_ref,
    attn_gain_ref,
    latent_gain_ref,
    ffn_gain_ref,
    w_query_ref,
    w_latent_ref,
    w_rope_key_ref,
    w_key_up_ref,
    w_value_up_ref,
    w_out_ref,
    latent_cache_ref,
    rope_cache_ref,
    w_up_ref,
    w_down_ref,
    out_ref,
    lengths_ref,
    ids_ref,
    weights_ref,
    hidden_in,
    attn_gain,
    latent_gain,
    ffn_gain,
    w_query,
    w_latent,
    w_rope_key,
    w_key_up,
    w_value_up,
    w_out,
    latents,
    ropes,
    residual,
    query_latent,
    query_rope,
    self_scores,
    scores,
    mixed_latent,
    part_out,
    w_up,
    w_down,
    part_in,
    middle,
    table,
    tables,
    own,
    rows_all,
    pick,
    mix,
    packed,
    lifted,
    activated,
    sum_out,
    pair_in,
    pair_sum,
    plane_in,
    plane_sum,
    line_in,
    own_out,
    finished,
    early_sem,
    cache_sem,
    up_sem,
    down_sem,
    part_send,
    part_recv,
    table_send,
    table_recv,
    line_send,
    line_recv,
    plane_send,
    plane_recv,
    pair_send,
    pair_recv,
    back_pair_send,
    back_pair_recv,
    back_plane_send,
    back_plane_recv,
    back_line_send,
    back_line_recv,
    done_send,
    done_recv,
    finish_sem,
):
    section = lax.axis_index("section")
    dev = lax.axis_index("dev")
    core = lax.rem(dev, 2)
    line = dev // 2
    pairs = devices // 2
    total = sections * devices
    me = dev * sections + section
    local, _, units, width = w_up.shape
    out_chunks, quarter, out_span = own.shape
    chunks, span = pair_sum.shape[0], pair_sum.shape[-1]
    rows = total * quarter
    experts = tables.shape[-1] // 2
    slots = packed.shape[0] // local
    bf16, f32 = jnp.bfloat16, jnp.float32
    partner = (section, dev + 1 - 2 * core)

    def remote(source, landing, send, recv, device):
        return pltpu.make_async_remote_copy(
            src_ref=source,
            dst_ref=landing,
            send_sem=send,
            recv_sem=recv,
            device_id=device,
            device_id_type=MESH,
        )

    def up_copy(e):
        return pltpu.make_async_copy(w_up_ref.at[e], w_up.at[e], up_sem.at[e])

    def down_copy(e):
        return pltpu.make_async_copy(w_down_ref.at[e], w_down.at[e], down_sem.at[e])

    heads, latent, nope = w_key_up.shape
    row_count, slots_kept, _ = latents.shape
    rope = w_rope_key.shape[0]
    padded = scores.shape[0] // row_count
    groups = cache_sem.shape[0] // 2
    group = row_count // groups
    score_scale = (nope + rope) ** (-0.5)
    flat = (((1,), (1,)), ((), ()))

    def early_copy(source, landing, n):
        return pltpu.make_async_copy(source, landing, early_sem.at[n])

    query_copy = early_copy(w_query_ref, w_query, 0)
    key_up_copy = early_copy(w_key_up_ref, w_key_up, 1)
    latent_copy = early_copy(w_latent_ref, w_latent, 2)
    rope_key_copy = early_copy(w_rope_key_ref, w_rope_key, 3)
    value_up_copy = early_copy(w_value_up_ref, w_value_up, 4)
    out_copy = early_copy(w_out_ref, w_out, 5)

    def cache_copies(g):
        held = pl.ds(g * group, group)
        return (
            pltpu.make_async_copy(latent_cache_ref.at[held], latents.at[held], cache_sem.at[2 * g]),
            pltpu.make_async_copy(rope_cache_ref.at[held], ropes.at[held], cache_sem.at[2 * g + 1]),
        )

    hidden_copy = early_copy(hidden_ref, hidden_in, 6)
    small_copies = (
        early_copy(attn_gain_ref, attn_gain, 7),
        early_copy(latent_gain_ref, latent_gain, 8),
        early_copy(ffn_gain_ref, ffn_gain, 9),
        early_copy(lengths_in, lengths_ref, 10),
        early_copy(ids_in, ids_ref, 11),
        early_copy(weights_in, weights_ref, 12),
    )

    hidden_copy.start()
    for copy in small_copies:
        copy.start()
    query_copy.start()
    key_up_copy.start()
    latent_copy.start()
    rope_key_copy.start()
    for g in range(groups):
        for copy in cache_copies(g):
            copy.start()
    value_up_copy.start()
    out_copy.start()

    barrier = pltpu.get_barrier_semaphore()

    @pl.loop(1, total)
    def _(i):
        t = lax.rem(me + i, total)
        pl.semaphore_signal(
            barrier, inc=1, device_id=(lax.rem(t, sections), t // sections), device_id_type=MESH
        )

    for copy in small_copies:
        copy.wait()
    row = lax.broadcasted_iota(jnp.int32, (row_count, rope), 0)
    positions = jnp.zeros((row_count, rope), jnp.int32)
    for r in range(row_count):
        positions = jnp.where(row == r, lengths_ref[r], positions)
    cosine, sine = turn_of(positions, rope)
    hidden_copy.wait()
    hidden = hidden_in[...].astype(f32)
    residual[...] = hidden
    normed = rms_norm(hidden, attn_gain[...]).astype(bf16)
    query_latent[...] = jnp.zeros_like(query_latent)
    query_rope[...] = jnp.zeros_like(query_rope)
    self_scores[...] = jnp.zeros_like(self_scores)
    query_copy.wait()
    queries = jnp.dot(normed, w_query[...], preferred_element_type=f32).astype(bf16).astype(f32)
    rope_key_copy.wait()
    latent_copy.wait()
    key_raw = lax.dot_general(normed, w_rope_key[...], flat, preferred_element_type=f32)
    key_new = rotary(key_raw, cosine, sine).astype(bf16).astype(f32)
    latent_raw = jnp.dot(normed, w_latent[...], preferred_element_type=f32)
    latent_new = rms_norm(latent_raw, latent_gain[...]).astype(bf16).astype(f32)
    key_up_copy.wait()
    for h in range(heads):
        first = h * (nope + rope)
        turned = rotary(queries[:, first + nope : first + nope + rope], cosine, sine)
        turned = turned.astype(bf16).astype(f32)
        mapped = lax.dot_general(
            queries[:, first : first + nope].astype(bf16),
            w_key_up[h],
            flat,
            preferred_element_type=f32,
        )
        mapped = mapped.astype(bf16).astype(f32)
        query_latent[:, h, :] = mapped
        query_rope[:, h, :] = turned
        own_score = jnp.sum(mapped * latent_new, axis=1, keepdims=True) + jnp.sum(
            turned * key_new, axis=1, keepdims=True
        )
        self_scores[pl.ds(h, row_count, stride=padded), :] = jnp.broadcast_to(
            own_score * score_scale, (row_count, 128)
        )

    pl.semaphore_wait(barrier, total - 1)

    def place_of(t):
        return (lax.rem(t // sections, 2) * sections + lax.rem(t, sections)) * pairs + t // (
            2 * sections
        )

    here = place_of(me)
    route_rows(table, ids_ref, weights_ref, section * quarter, experts, here)
    tables[here] = table[...]

    def table_copy(i, landing):
        t = lax.rem(me + i, total)
        return remote(
            table,
            tables.at[landing],
            table_send.at[i],
            table_recv.at[landing],
            (lax.rem(t, sections), t // sections),
        )

    @pl.loop(1, total)
    def _(i):
        table_copy(i, here).start()

    position = lax.broadcasted_iota(jnp.int32, (padded, slots_kept), 1)

    def score_rows(g):
        for r in range(g * group, (g + 1) * group):
            found = lax.dot_general(
                query_latent[r].astype(bf16), latents[r], flat, preferred_element_type=f32
            ) + jnp.dot(query_rope[r].astype(bf16), ropes[r], preferred_element_type=f32)
            scores[r * padded : (r + 1) * padded, :] = jnp.where(
                position < lengths_ref[r], found * score_scale, far_below
            )

    def mix_rows(g):
        held = slice(g * group * padded, (g + 1) * group * padded)
        own_scores = self_scores[held, :1]
        peak = jnp.maximum(jnp.max(scores[held, :], axis=1, keepdims=True), own_scores)
        likely = jnp.exp(scores[held, :] - peak)
        own_likely = jnp.exp(own_scores - peak)
        totals = jnp.sum(likely, axis=1, keepdims=True) + own_likely
        probs = (likely / totals).astype(bf16)
        own_probs = (own_likely / totals).astype(bf16).astype(f32)
        self_scores[held, :] = jnp.broadcast_to(own_probs, (group * padded, 128))
        for n in range(group):
            r = g * group + n
            mixed_latent[r] = jnp.dot(
                probs[n * padded : (n + 1) * padded, :], latents[r], preferred_element_type=f32
            )

    for g in range(groups):
        for copy in cache_copies(g):
            copy.wait()
        for e in range(g * local // groups, (g + 1) * local // groups):
            up_copy(e).start()
        score_rows(g)
        if g > 0:
            mix_rows(g - 1)
    for e in range(local):
        down_copy(e).start()
    mix_rows(groups - 1)

    value_up_copy.wait()
    head_outs = []
    for h in range(heads):
        rows_of = pl.ds(h, row_count, stride=padded)
        mixed = mixed_latent[:, h, :] + self_scores[rows_of, :][:, :1] * latent_new
        head_outs.append(
            jnp.dot(mixed.astype(bf16), w_value_up[h], preferred_element_type=f32).astype(bf16)
        )
    out_copy.wait()
    part = jnp.dot(jnp.concatenate(head_outs, axis=1), w_out[...], preferred_element_type=f32)
    for t in range(sections):
        part_out[t] = part[t * quarter : (t + 1) * quarter, :].astype(bf16)

    def part_copy(i, here):
        t = lax.rem(section + i, sections)
        return remote(part_out.at[t], part_in.at[here], part_send.at[i], part_recv.at[here], (t, dev))

    for i in range(1, sections):
        part_copy(i, section).start()

    mine = pl.ds(pl.multiple_of(section * quarter, quarter), quarter)
    summed = residual[mine, :] + part_out[section].astype(f32)
    for i in range(1, sections):
        t = lax.rem(section + i, sections)
        part_copy(i, t).wait_recv()
        summed = summed + part_in[t].astype(f32)
    middle_rows = summed.astype(bf16).astype(f32)
    middle[...] = middle_rows
    normed = rms_norm(middle_rows, ffn_gain[...]).astype(bf16)

    def line_copy(k, i, slot):
        t = lax.rem(line + i, pairs)
        return remote(
            own.at[k],
            rows_all.at[k, core, section, slot],
            line_send.at[k, i],
            line_recv.at[k, slot],
            (section, 2 * t + core),
        )

    def plane_copy(k, i, source, slot):
        block = rows_all.at[k, core, source, slot]
        return remote(
            block,
            block,
            plane_send.at[k, i, slot],
            plane_recv.at[k, source, slot],
            (lax.rem(section + i, sections), dev),
        )

    def pair_copy(k, which):
        return remote(
            rows_all.at[k, which], rows_all.at[k, which], pair_send.at[k], pair_recv.at[k], partner
        )

    for k in range(out_chunks):
        own[k] = normed[:, k * out_span : (k + 1) * out_span]
        rows_all[k, core, section, line] = normed[:, k * out_span : (k + 1) * out_span]

        @pl.loop(1, pairs)
        def _(i):
            line_copy(k, i, line).start()

    for k in range(out_chunks):
        for i in range(1, sections):
            plane_copy(k, i, section, line).start()
    for k in range(out_chunks):

        @pl.loop(1, pairs)
        def _(j):
            slot = lax.rem(line + j, pairs)
            line_copy(k, j, slot).wait_recv()
            for i in range(1, sections):
                plane_copy(k, i, section, slot).start()

    @pl.loop(1, total)
    def _(i):
        table_copy(i, place_of(lax.rem(me + i, total))).wait_recv()

    known = tables[...].reshape(rows, 2 * experts).astype(bf16)
    wide = local * slots
    column = lax.broadcasted_iota(jnp.int32, (2 * experts, wide), 1).astype(f32)
    column_expert = jnp.floor((column + 0.5) * (1.0 / slots))
    entry = lax.broadcasted_iota(jnp.int32, (2 * experts, wide), 0)
    entry = (entry - dev * local).astype(f32)
    weight_pick = jnp.where(entry == column_expert, 1.0, 0.0).astype(bf16)
    slot_pick = jnp.where(entry == column_expert + float(experts), 1.0, 0.0).astype(bf16)
    slot_map = jnp.dot(known, slot_pick, preferred_element_type=f32)
    weight_map = jnp.dot(known, weight_pick, preferred_element_type=f32)
    column = lax.broadcasted_iota(jnp.int32, (rows, wide), 1).astype(f32)
    chosen = slot_map == column - jnp.floor((column + 0.5) * (1.0 / slots)) * slots
    pick[...] = jnp.where(chosen, 1.0, 0.0).astype(bf16)
    mix[...] = jnp.where(chosen, weight_map, 0.0).astype(bf16)

    def to_partner(k):
        @pl.loop(0, pairs)
        def _(j):
            slot = lax.rem(line + j, pairs)
            for i in range(1, sections):
                plane_copy(k, i, lax.rem(section + i, sections), slot).wait_recv()

        pair_copy(k, core).start()

    to_partner(0)
    for k in range(out_chunks):
        if k + 1 < out_chunks:
            to_partner(k + 1)
        pair_copy(k, 1 - core).wait_recv()
        block = rows_all[k].astype(f32).reshape(rows, out_span).astype(bf16)
        packed[...] = lax.dot_general(
            pick[...], block, (((0,), (0,)), ((), ())), preferred_element_type=f32
        ).astype(bf16)
        for e in range(local):
            if k == 0:
                up_copy(e).wait()
            held = slice(e * slots, (e + 1) * slots)
            both = lax.dot_general(
                packed[held, :],
                w_up[e, :, :, k * out_span : (k + 1) * out_span].reshape(2 * units, out_span),
                flat,
                preferred_element_type=f32,
            )
            if k > 0:
                both = both + lifted[held, :]
            if k + 1 < out_chunks:
                lifted[held, :] = both
            else:
                gate, lift = both[:, :units], both[:, units:]
                activated[held, :] = (gate / (1.0 + jnp.exp(-gate)) * lift).astype(bf16)

    def back_pair_copy(k, which):
        return remote(
            sum_out.at[k, which], pair_in.at[k], back_pair_send.at[k], back_pair_recv.at[k], partner
        )

    def back_plane_copy(k, i, landing, slot):
        t = lax.rem(section + i, sections)
        return remote(
            pair_sum.at[k, t, slot],
            plane_in.at[k, landing, slot],
            back_plane_send.at[k, i, slot],
            back_plane_recv.at[k, landing, slot],
            (t, dev),
        )

    def back_line_copy(k, i, landing):
        t = lax.rem(line + i, pairs)
        return remote(
            plane_sum.at[k, t],
            line_in.at[k, landing],
            back_line_send.at[k, i],
            back_line_recv.at[k, landing],
            (section, 2 * t + core),
        )

    def done_copy(k, i, landing):
        return remote(
            own_out.at[k],
            finished.at[k, landing],
            done_send.at[k, i],
            done_recv.at[k, landing],
            (lax.rem(section + i, sections), dev),
        )

    def over_plane(k):
        back_pair_copy(k, 1 - core).wait_recv()
        pair_sum[k] = (sum_out[k, core].astype(f32) + pair_in[k].astype(f32)).astype(bf16)

        @pl.loop(1, pairs)
        def _(j):
            for i in range(1, sections):
                back_plane_copy(k, i, section, lax.rem(line + j, pairs)).start()

    def plane_total(k, slot):
        added = pair_sum[k, section, slot].astype(f32)
        for i in range(1, sections):
            t = lax.rem(section + i, sections)
            back_plane_copy(k, i, t, slot).wait_recv()
            added = added + plane_in[k, t, slot].astype(f32)
        return added

    def over_line(k):
        @pl.loop(1, pairs)
        def _(j):
            slot = lax.rem(line + j, pairs)
            plane_sum[k, slot] = plane_total(k, slot).astype(bf16)
            back_line_copy(k, j, line).start()

    def over_sections(k):
        result = middle[:, k * span : (k + 1) * span] + plane_total(k, line)
        for i in range(1, pairs):
            slot = lax.rem(line + i, pairs)
            back_line_copy(k, i, slot).wait_recv()
            result = result + line_in[k, slot].astype(f32)
        own_out[k] = result.astype(bf16)
        finished[k, section] = result.astype(bf16)
        for i in range(1, sections):
            done_copy(k, i, section).start()

    for k in range(chunks):
        part_of = slice(k * span, (k + 1) * span)
        outs = []
        for e in range(local):
            if k == 0:
                down_copy(e).wait()
            held = slice(e * slots, (e + 1) * slots)
            outs.append(
                jnp.dot(
                    activated[held, :], w_down[e, :, part_of], preferred_element_type=f32
                ).astype(bf16)
            )
        mixed = jnp.dot(mix[...], jnp.concatenate(outs, axis=0), preferred_element_type=f32)
        sum_out[k] = mixed.reshape(2, sections, pairs, quarter, span).astype(bf16)
        back_pair_copy(k, 1 - core).start()
        if k > 0:
            over_plane(k - 1)
    over_plane(chunks - 1)
    for k in range(chunks):
        for i in range(1, sections):
            back_plane_copy(k, i, section, line).start()
    for k in range(chunks):
        over_line(k)
    for k in range(chunks):
        over_sections(k)

    def finish_copy(k):
        return pltpu.make_async_copy(
            finished.at[k], out_ref.at[:, :, pl.ds(k * span, span)], finish_sem.at[k]
        )

    for k in range(chunks):
        for i in range(1, sections):
            done_copy(k, i, lax.rem(section + i, sections)).wait_recv()
        finish_copy(k).start()

    for i in range(1, sections):
        part_copy(i, section).wait_send()

    @pl.loop(1, total)
    def _(i):
        table_copy(i, here).wait_send()

    for k in range(out_chunks):

        @pl.loop(1, pairs)
        def _(i):
            line_copy(k, i, line).wait_send()

        @pl.loop(0, pairs)
        def _(j):
            for i in range(1, sections):
                plane_copy(k, i, section, j).wait_send()

        pair_copy(k, core).wait_send()

    for k in range(chunks):

        @pl.loop(1, pairs)
        def _(i):
            back_line_copy(k, i, line).wait_send()

        @pl.loop(0, pairs)
        def _(j):
            for i in range(1, sections):
                back_plane_copy(k, i, section, j).wait_send()

        for i in range(1, sections):
            done_copy(k, i, section).wait_send()
        back_pair_copy(k, 1 - core).wait_send()
        finish_copy(k).wait()


def per_device(
    hidden,
    lengths,
    attn_gain,
    w_query,
    w_latent,
    latent_gain,
    w_rope_key,
    w_key_up,
    w_value_up,
    w_out,
    latent_cache,
    rope_cache,
    ffn_gain,
    expert_ids,
    route_weights,
    w_gate_up,
    w_down,
):
    sections = lax.axis_size("section")
    devices = lax.axis_size("dev")
    total = sections * devices
    pairs = devices // 2
    row_count, width = hidden.shape
    quarter = row_count // sections
    heads, latent, _ = w_key_up.shape
    rope, slots_kept = rope_cache.shape[1:]
    local, _, units, _ = w_gate_up.shape
    experts = local * devices
    slots = total * MOST
    rows = total * quarter
    out_chunks, chunks = OUT_CHUNKS, BACK_CHUNKS
    out_span, span = width // out_chunks, width // chunks
    groups = CACHE_GROUPS
    padded = -(-heads // 8) * 8
    bf16, f32 = jnp.bfloat16, jnp.float32
    anywhere = pl.BlockSpec(memory_space=pl.ANY)
    sems = lambda *count: pltpu.SemaphoreType.DMA(count)
    out = pl.pallas_call(
        functools.partial(layer_kernel, sections, devices),
        out_shape=jax.ShapeDtypeStruct((sections, quarter, width), bf16),
        in_specs=[anywhere] * 17,
        out_specs=anywhere,
        scratch_shapes=[
            pltpu.SMEM(lengths.shape, jnp.int32),
            pltpu.SMEM(expert_ids.shape[::-1], jnp.int32),
            pltpu.SMEM(route_weights.shape[::-1], f32),
            pltpu.VMEM(hidden.shape, bf16),
            pltpu.VMEM((1, width), f32),
            pltpu.VMEM((1, latent), f32),
            pltpu.VMEM((1, width), f32),
            pltpu.VMEM(w_query.shape, bf16),
            pltpu.VMEM(w_latent.shape, bf16),
            pltpu.VMEM(w_rope_key.shape, bf16),
            pltpu.VMEM(w_key_up.shape, bf16),
            pltpu.VMEM(w_value_up.shape, bf16),
            pltpu.VMEM(w_out.shape, bf16),
            pltpu.VMEM(latent_cache.shape, bf16),
            pltpu.VMEM(rope_cache.shape, bf16),
            pltpu.VMEM((row_count, width), f32),
            pltpu.VMEM((row_count, padded, latent), f32),
            pltpu.VMEM((row_count, padded, rope), f32),
            pltpu.VMEM((row_count * padded, 128), f32),
            pltpu.VMEM((row_count * padded, slots_kept), f32),
            pltpu.VMEM((row_count, padded, latent), f32),
            pltpu.VMEM((sections, quarter, width), bf16),
            pltpu.VMEM(w_gate_up.shape, bf16),
            pltpu.VMEM(w_down.shape, bf16),
            pltpu.VMEM((sections, quarter, width), bf16),
            pltpu.VMEM((quarter, width), f32),
            pltpu.VMEM((quarter, 2 * experts), f32),
            pltpu.VMEM((total, quarter, 2 * experts), f32),
            pltpu.VMEM((out_chunks, quarter, out_span), bf16),
            pltpu.VMEM((out_chunks, 2, sections, pairs, quarter, out_span), bf16),
            pltpu.VMEM((rows, local * slots), bf16),
            pltpu.VMEM((rows, local * slots), bf16),
            pltpu.VMEM((local * slots, out_span), bf16),
            pltpu.VMEM((local * slots, 2 * units), f32),
            pltpu.VMEM((local * slots, units), bf16),
            pltpu.VMEM((chunks, 2, sections, pairs, quarter, span), bf16),
            pltpu.VMEM((chunks, sections, pairs, quarter, span), bf16),
            pltpu.VMEM((chunks, sections, pairs, quarter, span), bf16),
            pltpu.VMEM((chunks, sections, pairs, quarter, span), bf16),
            pltpu.VMEM((chunks, pairs, quarter, span), bf16),
            pltpu.VMEM((chunks, pairs, quarter, span), bf16),
            pltpu.VMEM((chunks, quarter, span), bf16),
            pltpu.VMEM((chunks, sections, quarter, span), bf16),
            sems(13),
            sems(2 * groups),
            sems(local),
            sems(local),
            sems(sections),
            sems(sections),
            sems(total),
            sems(total),
            sems(out_chunks, pairs),
            sems(out_chunks, pairs),
            sems(out_chunks, sections, pairs),
            sems(out_chunks, sections, pairs),
            sems(out_chunks),
            sems(out_chunks),
            sems(chunks),
            sems(chunks),
            sems(chunks, sections, pairs),
            sems(chunks, sections, pairs),
            sems(chunks, pairs),
            sems(chunks, pairs),
            sems(chunks, sections),
            sems(chunks, sections),
            sems(chunks),
        ],
        compiler_params=pltpu.CompilerParams(
            collective_id=0, has_side_effects=True, vmem_limit_bytes=63 * 1024 * 1024
        ),
    )(
        lengths,
        expert_ids.T,
        route_weights.T,
        hidden,
        attn_gain.reshape(1, width),
        latent_gain.reshape(1, latent),
        ffn_gain.reshape(1, width),
        w_query,
        w_latent,
        w_rope_key,
        w_key_up,
        w_value_up,
        w_out,
        latent_cache,
        rope_cache,
        w_gate_up,
        w_down,
    )
    return out.reshape(row_count, width)


def solution(mesh):
    in_specs = (
        P("dev", None),
        P("dev"),
        P(),
        P(None, "section"),
        P(),
        P(),
        P(),
        P("section", None, None),
        P("section", None, None),
        P("section", None),
        P("dev", None, None),
        P("dev", None, None),
        P(),
        P("dev", None),
        P("dev", None),
        P("dev", None, "section", None),
        P("dev", "section", None),
    )
    out_specs = P("dev", None)
    return jax.shard_map(
        per_device, mesh=mesh, in_specs=in_specs, out_specs=out_specs, check_vma=False
    )
```

```python
import functools

import jax
import jax.numpy as jnp
from jax import lax
from jax.experimental import pallas as pl
from jax.experimental.pallas import tpu as pltpu
from jax.sharding import PartitionSpec as P

MOST = 2
OUT_CHUNKS = 4
BACK_CHUNKS = 4
CACHE_GROUPS = 4
MESH = pl.DeviceIdType.MESH


epsilon = 1e-06
far_below = -1e30


def rms_norm(values, norm_gain):
    mean_square = jnp.mean(values * values, axis=-1, keepdims=True)
    return values * lax.rsqrt(mean_square + epsilon) * norm_gain


def turn_of(positions, width):
    half = width // 2
    step = lax.broadcasted_iota(jnp.int32, (1, width), 1)
    step = jnp.where(step < half, step, step - half).astype(jnp.float32)
    frequency = jnp.exp(-jnp.log(10000.0) * step / half)
    angles = positions.astype(jnp.float32) * frequency
    return jnp.cos(angles), jnp.sin(angles)


def rotary(values, cosine, sine):
    half = values.shape[-1] // 2
    turned = jnp.concatenate([-values[:, half:], values[:, :half]], axis=1)
    return values * cosine + turned * sine


def route_rows(table_ref, ids_ref, weights_ref, first_row, experts, place):
    rows = table_ref.shape[0]
    lane = lax.broadcasted_iota(jnp.int32, (rows, experts), 1)
    row = lax.broadcasted_iota(jnp.int32, (rows, experts), 0)
    dense = jnp.zeros((rows, experts), jnp.float32)
    routed = jnp.zeros((rows, experts), jnp.float32)
    for i in range(rows):
        for k in range(ids_ref.shape[0]):
            hit = (row == i) & (lane == ids_ref[k, first_row + i])
            dense = jnp.where(hit, weights_ref[k, first_row + i], dense)
            routed = jnp.where(hit, 1.0, routed)
    rank = jnp.zeros((rows, experts), jnp.float32)
    for j in range(rows - 1):
        rank = rank + jnp.where(row > j, routed[j : j + 1, :], 0.0)
    first = (place * MOST).astype(jnp.float32)
    table_ref[:, :experts] = dense
    table_ref[:, experts:] = jnp.where(routed > 0.0, first + rank, -1.0)


def layer_kernel(
    sections,
    devices,
    lengths_in,
    ids_in,
    weights_in,
    hidden_ref,
    attn_gain_ref,
    latent_gain_ref,
    ffn_gain_ref,
    w_query_ref,
    w_latent_ref,
    w_rope_key_ref,
    w_key_up_ref,
    w_value_up_ref,
    w_out_ref,
    latent_cache_ref,
    rope_cache_ref,
    w_up_ref,
    w_down_ref,
    out_ref,
    lengths_ref,
    ids_ref,
    weights_ref,
    hidden_in,
    attn_gain,
    latent_gain,
    ffn_gain,
    w_query,
    w_latent,
    w_rope_key,
    w_key_up,
    w_value_up,
    w_out,
    latents,
    ropes,
    residual,
    query_latent,
    query_rope,
    self_scores,
    scores,
    mixed_latent,
    part_out,
    w_up,
    w_down,
    part_in,
    middle,
    table,
    tables,
    own,
    rows_all,
    pick,
    mix,
    packed,
    lifted,
    activated,
    sum_out,
    pair_in,
    pair_sum,
    plane_in,
    plane_sum,
    line_in,
    own_out,
    finished,
    early_sem,
    cache_sem,
    up_sem,
    down_sem,
    part_send,
    part_recv,
    table_send,
    table_recv,
    line_send,
    line_recv,
    plane_send,
    plane_recv,
    pair_send,
    pair_recv,
    back_pair_send,
    back_pair_recv,
    back_plane_send,
    back_plane_recv,
    back_line_send,
    back_line_recv,
    done_send,
    done_recv,
    finish_sem,
):
    section = lax.axis_index("section")
    dev = lax.axis_index("dev")
    core = lax.rem(dev, 2)
    line = dev // 2
    pairs = devices // 2
    total = sections * devices
    me = dev * sections + section
    local, _, units, width = w_up.shape
    out_chunks, quarter, out_span = own.shape
    chunks, span = pair_sum.shape[0], pair_sum.shape[-1]
    rows = total * quarter
    experts = tables.shape[-1] // 2
    slots = packed.shape[0] // local
    bf16, f32 = jnp.bfloat16, jnp.float32
    partner = (section, dev + 1 - 2 * core)

    def remote(source, landing, send, recv, device):
        return pltpu.make_async_remote_copy(
            src_ref=source,
            dst_ref=landing,
            send_sem=send,
            recv_sem=recv,
            device_id=device,
            device_id_type=MESH,
        )

    def up_copy(e):
        return pltpu.make_async_copy(w_up_ref.at[e], w_up.at[e], up_sem.at[e])

    def down_copy(e):
        return pltpu.make_async_copy(w_down_ref.at[e], w_down.at[e], down_sem.at[e])

    heads, latent, nope = w_key_up.shape
    row_count, slots_kept, _ = latents.shape
    rope = w_rope_key.shape[0]
    padded = scores.shape[0] // row_count
    groups = cache_sem.shape[0] // 2
    group = row_count // groups
    score_scale = (nope + rope) ** (-0.5)
    flat = (((1,), (1,)), ((), ()))

    def early_copy(source, landing, n):
        return pltpu.make_async_copy(source, landing, early_sem.at[n])

    query_copy = early_copy(w_query_ref, w_query, 0)
    key_up_copy = early_copy(w_key_up_ref, w_key_up, 1)
    latent_copy = early_copy(w_latent_ref, w_latent, 2)
    rope_key_copy = early_copy(w_rope_key_ref, w_rope_key, 3)
    value_up_copy = early_copy(w_value_up_ref, w_value_up, 4)
    out_copy = early_copy(w_out_ref, w_out, 5)

    def cache_copies(g):
        held = pl.ds(g * group, group)
        return (
            pltpu.make_async_copy(latent_cache_ref.at[held], latents.at[held], cache_sem.at[2 * g]),
            pltpu.make_async_copy(rope_cache_ref.at[held], ropes.at[held], cache_sem.at[2 * g + 1]),
        )

    hidden_copy = early_copy(hidden_ref, hidden_in, 6)
    small_copies = (
        early_copy(attn_gain_ref, attn_gain, 7),
        early_copy(latent_gain_ref, latent_gain, 8),
        early_copy(ffn_gain_ref, ffn_gain, 9),
        early_copy(lengths_in, lengths_ref, 10),
        early_copy(ids_in, ids_ref, 11),
        early_copy(weights_in, weights_ref, 12),
    )

    hidden_copy.start()
    for copy in small_copies:
        copy.start()
    query_copy.start()
    key_up_copy.start()
    latent_copy.start()
    rope_key_copy.start()
    barrier = pltpu.get_barrier_semaphore()

    @pl.loop(1, total)
    def _(i):
        t = lax.rem(me + i, total)
        pl.semaphore_signal(
            barrier, inc=1, device_id=(lax.rem(t, sections), t // sections), device_id_type=MESH
        )

    for copy in small_copies:
        copy.wait()
    row = lax.broadcasted_iota(jnp.int32, (row_count, rope), 0)
    positions = jnp.zeros((row_count, rope), jnp.int32)
    for r in range(row_count):
        positions = jnp.where(row == r, lengths_ref[r], positions)
    cosine, sine = turn_of(positions, rope)
    hidden_copy.wait()
    hidden = hidden_in[...].astype(f32)
    residual[...] = hidden
    normed = rms_norm(hidden, attn_gain[...]).astype(bf16)
    query_latent[...] = jnp.zeros_like(query_latent)
    query_rope[...] = jnp.zeros_like(query_rope)
    self_scores[...] = jnp.zeros_like(self_scores)
    query_copy.wait()
    for g in range(groups):
        for copy in cache_copies(g):
            copy.start()
    value_up_copy.start()
    out_copy.start()
    queries = jnp.dot(normed, w_query[...], preferred_element_type=f32).astype(bf16).astype(f32)
    rope_key_copy.wait()
    latent_copy.wait()
    key_raw = lax.dot_general(normed, w_rope_key[...], flat, preferred_element_type=f32)
    key_new = rotary(key_raw, cosine, sine).astype(bf16).astype(f32)
    latent_raw = jnp.dot(normed, w_latent[...], preferred_element_type=f32)
    latent_new = rms_norm(latent_raw, latent_gain[...]).astype(bf16).astype(f32)
    key_up_copy.wait()
    for h in range(heads):
        first = h * (nope + rope)
        turned = rotary(queries[:, first + nope : first + nope + rope], cosine, sine)
        turned = turned.astype(bf16).astype(f32)
        mapped = lax.dot_general(
            queries[:, first : first + nope].astype(bf16),
            w_key_up[h],
            flat,
            preferred_element_type=f32,
        )
        mapped = mapped.astype(bf16).astype(f32)
        query_latent[:, h, :] = mapped
        query_rope[:, h, :] = turned
        own_score = jnp.sum(mapped * latent_new, axis=1, keepdims=True) + jnp.sum(
            turned * key_new, axis=1, keepdims=True
        )
        self_scores[pl.ds(h, row_count, stride=padded), :] = jnp.broadcast_to(
            own_score * score_scale, (row_count, 128)
        )

    pl.semaphore_wait(barrier, total - 1)

    def place_of(t):
        return (lax.rem(t // sections, 2) * sections + lax.rem(t, sections)) * pairs + t // (
            2 * sections
        )

    here = place_of(me)
    route_rows(table, ids_ref, weights_ref, section * quarter, experts, here)
    tables[here] = table[...]

    def table_copy(i, landing):
        t = lax.rem(me + i, total)
        return remote(
            table,
            tables.at[landing],
            table_send.at[i],
            table_recv.at[landing],
            (lax.rem(t, sections), t // sections),
        )

    @pl.loop(1, total)
    def _(i):
        table_copy(i, here).start()

    position = lax.broadcasted_iota(jnp.int32, (padded, slots_kept), 1)

    def score_rows(g):
        for r in range(g * group, (g + 1) * group):
            found = lax.dot_general(
                query_latent[r].astype(bf16), latents[r], flat, preferred_element_type=f32
            ) + jnp.dot(query_rope[r].astype(bf16), ropes[r], preferred_element_type=f32)
            scores[r * padded : (r + 1) * padded, :] = jnp.where(
                position < lengths_ref[r], found * score_scale, far_below
            )

    def mix_rows(g):
        held = slice(g * group * padded, (g + 1) * group * padded)
        own_scores = self_scores[held, :1]
        peak = jnp.maximum(jnp.max(scores[held, :], axis=1, keepdims=True), own_scores)
        likely = jnp.exp(scores[held, :] - peak)
        own_likely = jnp.exp(own_scores - peak)
        totals = jnp.sum(likely, axis=1, keepdims=True) + own_likely
        probs = (likely / totals).astype(bf16)
        own_probs = (own_likely / totals).astype(bf16).astype(f32)
        self_scores[held, :] = jnp.broadcast_to(own_probs, (group * padded, 128))
        for n in range(group):
            r = g * group + n
            mixed_latent[r] = jnp.dot(
                probs[n * padded : (n + 1) * padded, :], latents[r], preferred_element_type=f32
            )

    for g in range(groups):
        for copy in cache_copies(g):
            copy.wait()
        for e in range(g * local // groups, (g + 1) * local // groups):
            up_copy(e).start()
        score_rows(g)
        if g > 0:
            mix_rows(g - 1)
    for e in range(local):
        down_copy(e).start()
    mix_rows(groups - 1)

    value_up_copy.wait()
    head_outs = []
    for h in range(heads):
        rows_of = pl.ds(h, row_count, stride=padded)
        mixed = mixed_latent[:, h, :] + self_scores[rows_of, :][:, :1] * latent_new
        head_outs.append(
            jnp.dot(mixed.astype(bf16), w_value_up[h], preferred_element_type=f32).astype(bf16)
        )
    out_copy.wait()
    part = jnp.dot(jnp.concatenate(head_outs, axis=1), w_out[...], preferred_element_type=f32)
    for t in range(sections):
        part_out[t] = part[t * quarter : (t + 1) * quarter, :].astype(bf16)

    def part_copy(i, here):
        t = lax.rem(section + i, sections)
        return remote(part_out.at[t], part_in.at[here], part_send.at[i], part_recv.at[here], (t, dev))

    for i in range(1, sections):
        part_copy(i, section).start()

    mine = pl.ds(pl.multiple_of(section * quarter, quarter), quarter)
    summed = residual[mine, :] + part_out[section].astype(f32)
    for i in range(1, sections):
        t = lax.rem(section + i, sections)
        part_copy(i, t).wait_recv()
        summed = summed + part_in[t].astype(f32)
    middle_rows = summed.astype(bf16).astype(f32)
    middle[...] = middle_rows
    normed = rms_norm(middle_rows, ffn_gain[...]).astype(bf16)

    def line_copy(k, i, slot):
        t = lax.rem(line + i, pairs)
        return remote(
            own.at[k],
            rows_all.at[k, core, section, slot],
            line_send.at[k, i],
            line_recv.at[k, slot],
            (section, 2 * t + core),
        )

    def plane_copy(k, i, source, slot):
        block = rows_all.at[k, core, source, slot]
        return remote(
            block,
            block,
            plane_send.at[k, i, slot],
            plane_recv.at[k, source, slot],
            (lax.rem(section + i, sections), dev),
        )

    def pair_copy(k, which):
        return remote(
            rows_all.at[k, which], rows_all.at[k, which], pair_send.at[k], pair_recv.at[k], partner
        )

    for k in range(out_chunks):
        own[k] = normed[:, k * out_span : (k + 1) * out_span]
        rows_all[k, core, section, line] = normed[:, k * out_span : (k + 1) * out_span]

        @pl.loop(1, pairs)
        def _(i):
            line_copy(k, i, line).start()

    for k in range(out_chunks):
        for i in range(1, sections):
            plane_copy(k, i, section, line).start()
    for k in range(out_chunks):

        @pl.loop(1, pairs)
        def _(j):
            slot = lax.rem(line + j, pairs)
            line_copy(k, j, slot).wait_recv()
            for i in range(1, sections):
                plane_copy(k, i, section, slot).start()

    @pl.loop(1, total)
    def _(i):
        table_copy(i, place_of(lax.rem(me + i, total))).wait_recv()

    known = tables[...].reshape(rows, 2 * experts).astype(bf16)
    wide = local * slots
    column = lax.broadcasted_iota(jnp.int32, (2 * experts, wide), 1).astype(f32)
    column_expert = jnp.floor((column + 0.5) * (1.0 / slots))
    entry = lax.broadcasted_iota(jnp.int32, (2 * experts, wide), 0)
    entry = (entry - dev * local).astype(f32)
    weight_pick = jnp.where(entry == column_expert, 1.0, 0.0).astype(bf16)
    slot_pick = jnp.where(entry == column_expert + float(experts), 1.0, 0.0).astype(bf16)
    slot_map = jnp.dot(known, slot_pick, preferred_element_type=f32)
    weight_map = jnp.dot(known, weight_pick, preferred_element_type=f32)
    column = lax.broadcasted_iota(jnp.int32, (rows, wide), 1).astype(f32)
    chosen = slot_map == column - jnp.floor((column + 0.5) * (1.0 / slots)) * slots
    pick[...] = jnp.where(chosen, 1.0, 0.0).astype(bf16).T
    mix[...] = jnp.where(chosen, weight_map, 0.0).astype(bf16)

    def to_partner(k):
        @pl.loop(0, pairs)
        def _(j):
            slot = lax.rem(line + j, pairs)
            for i in range(1, sections):
                plane_copy(k, i, lax.rem(section + i, sections), slot).wait_recv()

        pair_copy(k, core).start()

    to_partner(0)
    for k in range(out_chunks):
        if k + 1 < out_chunks:
            to_partner(k + 1)
        pair_copy(k, 1 - core).wait_recv()
        block = rows_all[k].astype(f32).reshape(rows, out_span).astype(bf16)
        packed[...] = jnp.dot(pick[...], block, preferred_element_type=f32).astype(bf16)
        for e in range(local):
            if k == 0:
                up_copy(e).wait()
            held = slice(e * slots, (e + 1) * slots)
            both = lax.dot_general(
                packed[held, :],
                w_up[e, :, :, k * out_span : (k + 1) * out_span].reshape(2 * units, out_span),
                flat,
                preferred_element_type=f32,
            )
            if k > 0:
                both = both + lifted[held, :]
            if k + 1 < out_chunks:
                lifted[held, :] = both
            else:
                gate, lift = both[:, :units], both[:, units:]
                activated[held, :] = (gate / (1.0 + jnp.exp(-gate)) * lift).astype(bf16)

    def back_pair_copy(k, which):
        return remote(
            sum_out.at[k, which], pair_in.at[k], back_pair_send.at[k], back_pair_recv.at[k], partner
        )

    def back_plane_copy(k, i, landing, slot):
        t = lax.rem(section + i, sections)
        return remote(
            pair_sum.at[k, t, slot],
            plane_in.at[k, landing, slot],
            back_plane_send.at[k, i, slot],
            back_plane_recv.at[k, landing, slot],
            (t, dev),
        )

    def back_line_copy(k, i, landing):
        t = lax.rem(line + i, pairs)
        return remote(
            plane_sum.at[k, t],
            line_in.at[k, landing],
            back_line_send.at[k, i],
            back_line_recv.at[k, landing],
            (section, 2 * t + core),
        )

    def done_copy(k, i, landing):
        return remote(
            own_out.at[k],
            finished.at[k, landing],
            done_send.at[k, i],
            done_recv.at[k, landing],
            (lax.rem(section + i, sections), dev),
        )

    def over_plane(k):
        back_pair_copy(k, 1 - core).wait_recv()
        pair_sum[k] = (sum_out[k, core].astype(f32) + pair_in[k].astype(f32)).astype(bf16)

        @pl.loop(1, pairs)
        def _(j):
            for i in range(1, sections):
                back_plane_copy(k, i, section, lax.rem(line + j, pairs)).start()

    def plane_total(k, slot):
        added = pair_sum[k, section, slot].astype(f32)
        for i in range(1, sections):
            t = lax.rem(section + i, sections)
            back_plane_copy(k, i, t, slot).wait_recv()
            added = added + plane_in[k, t, slot].astype(f32)
        return added

    def over_line(k):
        @pl.loop(1, pairs)
        def _(j):
            slot = lax.rem(line + j, pairs)
            plane_sum[k, slot] = plane_total(k, slot).astype(bf16)
            back_line_copy(k, j, line).start()

    def over_sections(k):
        result = middle[:, k * span : (k + 1) * span] + plane_total(k, line)
        for i in range(1, pairs):
            slot = lax.rem(line + i, pairs)
            back_line_copy(k, i, slot).wait_recv()
            result = result + line_in[k, slot].astype(f32)
        own_out[k] = result.astype(bf16)
        finished[k, section] = result.astype(bf16)
        for i in range(1, sections):
            done_copy(k, i, section).start()

    for k in range(chunks):
        part_of = slice(k * span, (k + 1) * span)
        outs = []
        for e in range(local):
            if k == 0:
                down_copy(e).wait()
            held = slice(e * slots, (e + 1) * slots)
            outs.append(
                jnp.dot(
                    activated[held, :], w_down[e, :, part_of], preferred_element_type=f32
                ).astype(bf16)
            )
        mixed = jnp.dot(mix[...], jnp.concatenate(outs, axis=0), preferred_element_type=f32)
        sum_out[k] = mixed.reshape(2, sections, pairs, quarter, span).astype(bf16)
        back_pair_copy(k, 1 - core).start()
        if k > 0:
            over_plane(k - 1)
    over_plane(chunks - 1)
    for k in range(chunks):
        for i in range(1, sections):
            back_plane_copy(k, i, section, line).start()
    for k in range(chunks):
        over_line(k)
    for k in range(chunks):
        over_sections(k)

    def finish_copy(k):
        return pltpu.make_async_copy(
            finished.at[k], out_ref.at[:, :, pl.ds(k * span, span)], finish_sem.at[k]
        )

    for k in range(chunks):
        for i in range(1, sections):
            done_copy(k, i, lax.rem(section + i, sections)).wait_recv()
        finish_copy(k).start()

    for i in range(1, sections):
        part_copy(i, section).wait_send()

    @pl.loop(1, total)
    def _(i):
        table_copy(i, here).wait_send()

    for k in range(out_chunks):

        @pl.loop(1, pairs)
        def _(i):
            line_copy(k, i, line).wait_send()

        @pl.loop(0, pairs)
        def _(j):
            for i in range(1, sections):
                plane_copy(k, i, section, j).wait_send()

        pair_copy(k, core).wait_send()

    for k in range(chunks):

        @pl.loop(1, pairs)
        def _(i):
            back_line_copy(k, i, line).wait_send()

        @pl.loop(0, pairs)
        def _(j):
            for i in range(1, sections):
                back_plane_copy(k, i, section, j).wait_send()

        for i in range(1, sections):
            done_copy(k, i, section).wait_send()
        back_pair_copy(k, 1 - core).wait_send()
        finish_copy(k).wait()


def per_device(
    hidden,
    lengths,
    attn_gain,
    w_query,
    w_latent,
    latent_gain,
    w_rope_key,
    w_key_up,
    w_value_up,
    w_out,
    latent_cache,
    rope_cache,
    ffn_gain,
    expert_ids,
    route_weights,
    w_gate_up,
    w_down,
):
    sections = lax.axis_size("section")
    devices = lax.axis_size("dev")
    total = sections * devices
    pairs = devices // 2
    row_count, width = hidden.shape
    quarter = row_count // sections
    heads, latent, _ = w_key_up.shape
    rope, slots_kept = rope_cache.shape[1:]
    local, _, units, _ = w_gate_up.shape
    experts = local * devices
    slots = total * MOST
    rows = total * quarter
    out_chunks, chunks = OUT_CHUNKS, BACK_CHUNKS
    out_span, span = width // out_chunks, width // chunks
    groups = CACHE_GROUPS
    padded = -(-heads // 8) * 8
    bf16, f32 = jnp.bfloat16, jnp.float32
    anywhere = pl.BlockSpec(memory_space=pl.ANY)
    sems = lambda *count: pltpu.SemaphoreType.DMA(count)
    out = pl.pallas_call(
        functools.partial(layer_kernel, sections, devices),
        out_shape=jax.ShapeDtypeStruct((sections, quarter, width), bf16),
        in_specs=[anywhere] * 17,
        out_specs=anywhere,
        scratch_shapes=[
            pltpu.SMEM(lengths.shape, jnp.int32),
            pltpu.SMEM(expert_ids.shape[::-1], jnp.int32),
            pltpu.SMEM(route_weights.shape[::-1], f32),
            pltpu.VMEM(hidden.shape, bf16),
            pltpu.VMEM((1, width), f32),
            pltpu.VMEM((1, latent), f32),
            pltpu.VMEM((1, width), f32),
            pltpu.VMEM(w_query.shape, bf16),
            pltpu.VMEM(w_latent.shape, bf16),
            pltpu.VMEM(w_rope_key.shape, bf16),
            pltpu.VMEM(w_key_up.shape, bf16),
            pltpu.VMEM(w_value_up.shape, bf16),
            pltpu.VMEM(w_out.shape, bf16),
            pltpu.VMEM(latent_cache.shape, bf16),
            pltpu.VMEM(rope_cache.shape, bf16),
            pltpu.VMEM((row_count, width), f32),
            pltpu.VMEM((row_count, padded, latent), f32),
            pltpu.VMEM((row_count, padded, rope), f32),
            pltpu.VMEM((row_count * padded, 128), f32),
            pltpu.VMEM((row_count * padded, slots_kept), f32),
            pltpu.VMEM((row_count, padded, latent), f32),
            pltpu.VMEM((sections, quarter, width), bf16),
            pltpu.VMEM(w_gate_up.shape, bf16),
            pltpu.VMEM(w_down.shape, bf16),
            pltpu.VMEM((sections, quarter, width), bf16),
            pltpu.VMEM((quarter, width), f32),
            pltpu.VMEM((quarter, 2 * experts), f32),
            pltpu.VMEM((total, quarter, 2 * experts), f32),
            pltpu.VMEM((out_chunks, quarter, out_span), bf16),
            pltpu.VMEM((out_chunks, 2, sections, pairs, quarter, out_span), bf16),
            pltpu.VMEM((local * slots, rows), bf16),
            pltpu.VMEM((rows, local * slots), bf16),
            pltpu.VMEM((local * slots, out_span), bf16),
            pltpu.VMEM((local * slots, 2 * units), f32),
            pltpu.VMEM((local * slots, units), bf16),
            pltpu.VMEM((chunks, 2, sections, pairs, quarter, span), bf16),
            pltpu.VMEM((chunks, sections, pairs, quarter, span), bf16),
            pltpu.VMEM((chunks, sections, pairs, quarter, span), bf16),
            pltpu.VMEM((chunks, sections, pairs, quarter, span), bf16),
            pltpu.VMEM((chunks, pairs, quarter, span), bf16),
            pltpu.VMEM((chunks, pairs, quarter, span), bf16),
            pltpu.VMEM((chunks, quarter, span), bf16),
            pltpu.VMEM((chunks, sections, quarter, span), bf16),
            sems(13),
            sems(2 * groups),
            sems(local),
            sems(local),
            sems(sections),
            sems(sections),
            sems(total),
            sems(total),
            sems(out_chunks, pairs),
            sems(out_chunks, pairs),
            sems(out_chunks, sections, pairs),
            sems(out_chunks, sections, pairs),
            sems(out_chunks),
            sems(out_chunks),
            sems(chunks),
            sems(chunks),
            sems(chunks, sections, pairs),
            sems(chunks, sections, pairs),
            sems(chunks, pairs),
            sems(chunks, pairs),
            sems(chunks, sections),
            sems(chunks, sections),
            sems(chunks),
        ],
        compiler_params=pltpu.CompilerParams(
            collective_id=0, has_side_effects=True, vmem_limit_bytes=63 * 1024 * 1024
        ),
    )(
        lengths,
        expert_ids.T,
        route_weights.T,
        hidden,
        attn_gain.reshape(1, width),
        latent_gain.reshape(1, latent),
        ffn_gain.reshape(1, width),
        w_query,
        w_latent,
        w_rope_key,
        w_key_up,
        w_value_up,
        w_out,
        latent_cache,
        rope_cache,
        w_gate_up,
        w_down,
    )
    return out.reshape(row_count, width)


def solution(mesh):
    in_specs = (
        P("dev", None),
        P("dev"),
        P(),
        P(None, "section"),
        P(),
        P(),
        P(),
        P("section", None, None),
        P("section", None, None),
        P("section", None),
        P("dev", None, None),
        P("dev", None, None),
        P(),
        P("dev", None),
        P("dev", None),
        P("dev", None, "section", None),
        P("dev", "section", None),
    )
    out_specs = P("dev", None)
    return jax.shard_map(
        per_device, mesh=mesh, in_specs=in_specs, out_specs=out_specs, check_vma=False
    )
```

```python
import functools

import jax
import jax.numpy as jnp
from jax import lax
from jax.experimental import pallas as pl
from jax.experimental.pallas import tpu as pltpu
from jax.sharding import PartitionSpec as P

MOST = 2
OUT_CHUNKS = 4
BACK_CHUNKS = 4
CACHE_GROUPS = 4
MESH = pl.DeviceIdType.MESH


epsilon = 1e-06
far_below = -1e30


def rms_norm(values, norm_gain):
    mean_square = jnp.mean(values * values, axis=-1, keepdims=True)
    return values * lax.rsqrt(mean_square + epsilon) * norm_gain


def turn_of(positions, width):
    half = width // 2
    step = lax.broadcasted_iota(jnp.int32, (1, width), 1)
    step = jnp.where(step < half, step, step - half).astype(jnp.float32)
    frequency = jnp.exp(-jnp.log(10000.0) * step / half)
    angles = positions.astype(jnp.float32) * frequency
    return jnp.cos(angles), jnp.sin(angles)


def rotary(values, cosine, sine):
    half = values.shape[-1] // 2
    turned = jnp.concatenate([-values[:, half:], values[:, :half]], axis=1)
    return values * cosine + turned * sine


def route_rows(table_ref, ids_ref, weights_ref, first_row, experts, place):
    rows = table_ref.shape[0]
    lane = lax.broadcasted_iota(jnp.int32, (rows, experts), 1)
    row = lax.broadcasted_iota(jnp.int32, (rows, experts), 0)
    dense = jnp.zeros((rows, experts), jnp.float32)
    routed = jnp.zeros((rows, experts), jnp.float32)
    for i in range(rows):
        for k in range(ids_ref.shape[0]):
            hit = (row == i) & (lane == ids_ref[k, first_row + i])
            dense = jnp.where(hit, weights_ref[k, first_row + i], dense)
            routed = jnp.where(hit, 1.0, routed)
    rank = jnp.zeros((rows, experts), jnp.float32)
    for j in range(rows - 1):
        rank = rank + jnp.where(row > j, routed[j : j + 1, :], 0.0)
    first = (place * MOST).astype(jnp.float32)
    table_ref[:, :experts] = dense
    table_ref[:, experts:] = jnp.where(routed > 0.0, first + rank, -1.0)


def layer_kernel(
    sections,
    devices,
    lengths_in,
    ids_in,
    weights_in,
    hidden_ref,
    attn_gain_ref,
    latent_gain_ref,
    ffn_gain_ref,
    w_query_ref,
    w_latent_ref,
    w_rope_key_ref,
    w_key_up_ref,
    w_value_up_ref,
    w_out_ref,
    latent_cache_ref,
    rope_cache_ref,
    w_up_ref,
    w_down_ref,
    out_ref,
    lengths_ref,
    ids_ref,
    weights_ref,
    hidden_in,
    attn_gain,
    latent_gain,
    ffn_gain,
    w_query,
    w_latent,
    w_rope_key,
    w_key_up,
    w_value_up,
    w_out,
    latents,
    ropes,
    residual,
    query_latent,
    query_rope,
    self_scores,
    scores,
    mixed_latent,
    part_out,
    w_up,
    w_down,
    part_in,
    middle,
    table,
    tables,
    own,
    rows_all,
    pick,
    mix,
    packed,
    lifted,
    activated,
    sum_out,
    pair_in,
    pair_sum,
    plane_in,
    plane_sum,
    line_in,
    own_out,
    finished,
    early_sem,
    cache_sem,
    up_sem,
    down_sem,
    part_send,
    part_recv,
    table_send,
    table_recv,
    line_send,
    line_recv,
    plane_send,
    plane_recv,
    pair_send,
    pair_recv,
    back_pair_send,
    back_pair_recv,
    back_plane_send,
    back_plane_recv,
    back_line_send,
    back_line_recv,
    done_send,
    done_recv,
    finish_sem,
):
    section = lax.axis_index("section")
    dev = lax.axis_index("dev")
    core = lax.rem(dev, 2)
    line = dev // 2
    pairs = devices // 2
    total = sections * devices
    me = dev * sections + section
    local, _, units, width = w_up.shape
    out_chunks, quarter, out_span = own.shape
    chunks, span = pair_sum.shape[0], pair_sum.shape[-1]
    rows = total * quarter
    experts = tables.shape[-1] // 2
    slots = packed.shape[0] // local
    bf16, f32 = jnp.bfloat16, jnp.float32
    partner = (section, dev + 1 - 2 * core)

    def remote(source, landing, send, recv, device):
        return pltpu.make_async_remote_copy(
            src_ref=source,
            dst_ref=landing,
            send_sem=send,
            recv_sem=recv,
            device_id=device,
            device_id_type=MESH,
        )

    def up_copy(e):
        return pltpu.make_async_copy(w_up_ref.at[e], w_up.at[e], up_sem.at[e])

    def down_copy(e):
        return pltpu.make_async_copy(w_down_ref.at[e], w_down.at[e], down_sem.at[e])

    heads, latent, nope = w_key_up.shape
    row_count, slots_kept, _ = latents.shape
    rope = w_rope_key.shape[0]
    padded = scores.shape[0] // row_count
    groups = cache_sem.shape[0] // 2
    group = row_count // groups
    score_scale = (nope + rope) ** (-0.5)
    flat = (((1,), (1,)), ((), ()))

    def early_copy(source, landing, n):
        return pltpu.make_async_copy(source, landing, early_sem.at[n])

    query_copy = early_copy(w_query_ref, w_query, 0)
    key_up_copy = early_copy(w_key_up_ref, w_key_up, 1)
    latent_copy = early_copy(w_latent_ref, w_latent, 2)
    rope_key_copy = early_copy(w_rope_key_ref, w_rope_key, 3)
    value_up_copy = early_copy(w_value_up_ref, w_value_up, 4)
    out_copy = early_copy(w_out_ref, w_out, 5)

    def cache_copies(g):
        held = pl.ds(g * group, group)
        return (
            pltpu.make_async_copy(latent_cache_ref.at[held], latents.at[held], cache_sem.at[2 * g]),
            pltpu.make_async_copy(rope_cache_ref.at[held], ropes.at[held], cache_sem.at[2 * g + 1]),
        )

    hidden_copy = early_copy(hidden_ref, hidden_in, 6)
    small_copies = (
        early_copy(attn_gain_ref, attn_gain, 7),
        early_copy(latent_gain_ref, latent_gain, 8),
        early_copy(ffn_gain_ref, ffn_gain, 9),
        early_copy(lengths_in, lengths_ref, 10),
        early_copy(ids_in, ids_ref, 11),
        early_copy(weights_in, weights_ref, 12),
    )

    hidden_copy.start()
    for copy in small_copies:
        copy.start()
    query_copy.start()
    key_up_copy.start()
    latent_copy.start()
    rope_key_copy.start()
    barrier = pltpu.get_barrier_semaphore()

    @pl.loop(1, total)
    def _(i):
        t = lax.rem(me + i, total)
        pl.semaphore_signal(
            barrier, inc=1, device_id=(lax.rem(t, sections), t // sections), device_id_type=MESH
        )

    for copy in small_copies:
        copy.wait()
    row = lax.broadcasted_iota(jnp.int32, (row_count, rope), 0)
    positions = jnp.zeros((row_count, rope), jnp.int32)
    for r in range(row_count):
        positions = jnp.where(row == r, lengths_ref[r], positions)
    cosine, sine = turn_of(positions, rope)
    hidden_copy.wait()
    hidden = hidden_in[...].astype(f32)
    residual[...] = hidden
    normed = rms_norm(hidden, attn_gain[...]).astype(bf16)
    query_latent[...] = jnp.zeros_like(query_latent)
    query_rope[...] = jnp.zeros_like(query_rope)
    self_scores[...] = jnp.zeros_like(self_scores)
    query_copy.wait()
    for g in range(groups):
        for copy in cache_copies(g):
            copy.start()
    value_up_copy.start()
    out_copy.start()
    queries = jnp.dot(normed, w_query[...], preferred_element_type=f32).astype(bf16).astype(f32)
    rope_key_copy.wait()
    latent_copy.wait()
    key_raw = lax.dot_general(normed, w_rope_key[...], flat, preferred_element_type=f32)
    key_new = rotary(key_raw, cosine, sine).astype(bf16).astype(f32)
    latent_raw = jnp.dot(normed, w_latent[...], preferred_element_type=f32)
    latent_new = rms_norm(latent_raw, latent_gain[...]).astype(bf16).astype(f32)
    key_up_copy.wait()
    for h in range(heads):
        first = h * (nope + rope)
        turned = rotary(queries[:, first + nope : first + nope + rope], cosine, sine)
        turned = turned.astype(bf16).astype(f32)
        mapped = lax.dot_general(
            queries[:, first : first + nope].astype(bf16),
            w_key_up[h],
            flat,
            preferred_element_type=f32,
        )
        mapped = mapped.astype(bf16).astype(f32)
        query_latent[:, h, :] = mapped
        query_rope[:, h, :] = turned
        own_score = jnp.sum(mapped * latent_new, axis=1, keepdims=True) + jnp.sum(
            turned * key_new, axis=1, keepdims=True
        )
        self_scores[pl.ds(h, row_count, stride=padded), :] = jnp.broadcast_to(
            own_score * score_scale, (row_count, 128)
        )

    pl.semaphore_wait(barrier, total - 1)

    def place_of(t):
        return (lax.rem(t // sections, 2) * sections + lax.rem(t, sections)) * pairs + t // (
            2 * sections
        )

    here = place_of(me)
    route_rows(table, ids_ref, weights_ref, section * quarter, experts, here)
    tables[here] = table[...]

    def table_copy(i, landing):
        t = lax.rem(me + i, total)
        return remote(
            table,
            tables.at[landing],
            table_send.at[i],
            table_recv.at[landing],
            (lax.rem(t, sections), t // sections),
        )

    @pl.loop(1, total)
    def _(i):
        table_copy(i, here).start()

    position = lax.broadcasted_iota(jnp.int32, (padded, slots_kept), 1)

    def score_rows(g):
        for r in range(g * group, (g + 1) * group):
            found = lax.dot_general(
                query_latent[r].astype(bf16), latents[r], flat, preferred_element_type=f32
            ) + jnp.dot(query_rope[r].astype(bf16), ropes[r], preferred_element_type=f32)
            scores[r * padded : (r + 1) * padded, :] = jnp.where(
                position < lengths_ref[r], found * score_scale, far_below
            )

    def mix_rows(g):
        held = slice(g * group * padded, (g + 1) * group * padded)
        own_scores = self_scores[held, :1]
        peak = jnp.maximum(jnp.max(scores[held, :], axis=1, keepdims=True), own_scores)
        likely = jnp.exp(scores[held, :] - peak)
        own_likely = jnp.exp(own_scores - peak)
        totals = jnp.sum(likely, axis=1, keepdims=True) + own_likely
        probs = (likely / totals).astype(bf16)
        own_probs = (own_likely / totals).astype(bf16).astype(f32)
        self_scores[held, :] = jnp.broadcast_to(own_probs, (group * padded, 128))
        for n in range(group):
            r = g * group + n
            mixed_latent[r] = jnp.dot(
                probs[n * padded : (n + 1) * padded, :], latents[r], preferred_element_type=f32
            )

    for g in range(groups):
        for copy in cache_copies(g):
            copy.wait()
        for e in range(g * local // groups, (g + 1) * local // groups):
            up_copy(e).start()
        score_rows(g)
        if g > 0:
            mix_rows(g - 1)
    for e in range(local):
        down_copy(e).start()
    mix_rows(groups - 1)

    value_up_copy.wait()
    head_outs = []
    for h in range(heads):
        rows_of = pl.ds(h, row_count, stride=padded)
        mixed = mixed_latent[:, h, :] + self_scores[rows_of, :][:, :1] * latent_new
        head_outs.append(
            jnp.dot(mixed.astype(bf16), w_value_up[h], preferred_element_type=f32).astype(bf16)
        )
    out_copy.wait()
    part = jnp.dot(jnp.concatenate(head_outs, axis=1), w_out[...], preferred_element_type=f32)
    for t in range(sections):
        part_out[t] = part[t * quarter : (t + 1) * quarter, :].astype(bf16)

    def part_copy(i, here):
        t = lax.rem(section + i, sections)
        return remote(part_out.at[t], part_in.at[here], part_send.at[i], part_recv.at[here], (t, dev))

    for i in range(1, sections):
        part_copy(i, section).start()

    mine = pl.ds(pl.multiple_of(section * quarter, quarter), quarter)
    summed = residual[mine, :] + part_out[section].astype(f32)
    for i in range(1, sections):
        t = lax.rem(section + i, sections)
        part_copy(i, t).wait_recv()
        summed = summed + part_in[t].astype(f32)
    middle_rows = summed.astype(bf16).astype(f32)
    middle[...] = middle_rows
    normed = rms_norm(middle_rows, ffn_gain[...]).astype(bf16)

    def line_copy(k, i, slot):
        t = lax.rem(line + i, pairs)
        return remote(
            own.at[k],
            rows_all.at[k, core, section, slot],
            line_send.at[k, i],
            line_recv.at[k, slot],
            (section, 2 * t + core),
        )

    def plane_copy(k, i, source, slot):
        block = rows_all.at[k, core, source, slot]
        return remote(
            block,
            block,
            plane_send.at[k, i, slot],
            plane_recv.at[k, source, slot],
            (lax.rem(section + i, sections), dev),
        )

    def pair_copy(k, which):
        return remote(
            rows_all.at[k, which], rows_all.at[k, which], pair_send.at[k], pair_recv.at[k], partner
        )

    for k in range(out_chunks):
        own[k] = normed[:, k * out_span : (k + 1) * out_span]
        rows_all[k, core, section, line] = normed[:, k * out_span : (k + 1) * out_span]

        @pl.loop(1, pairs)
        def _(i):
            line_copy(k, i, line).start()

    for k in range(out_chunks):
        for i in range(1, sections):
            plane_copy(k, i, section, line).start()
    for k in range(out_chunks):

        @pl.loop(1, pairs)
        def _(j):
            slot = lax.rem(line + j, pairs)
            line_copy(k, j, slot).wait_recv()
            for i in range(1, sections):
                plane_copy(k, i, section, slot).start()

    @pl.loop(1, total)
    def _(i):
        table_copy(i, place_of(lax.rem(me + i, total))).wait_recv()

    known = tables[...].reshape(rows, 2 * experts).astype(bf16)
    wide = local * slots
    column = lax.broadcasted_iota(jnp.int32, (2 * experts, wide), 1).astype(f32)
    column_expert = jnp.floor((column + 0.5) * (1.0 / slots))
    entry = lax.broadcasted_iota(jnp.int32, (2 * experts, wide), 0)
    entry = (entry - dev * local).astype(f32)
    weight_pick = jnp.where(entry == column_expert, 1.0, 0.0).astype(bf16)
    slot_pick = jnp.where(entry == column_expert + float(experts), 1.0, 0.0).astype(bf16)
    slot_map = jnp.dot(known, slot_pick, preferred_element_type=f32)
    weight_map = jnp.dot(known, weight_pick, preferred_element_type=f32)
    column = lax.broadcasted_iota(jnp.int32, (rows, wide), 1).astype(f32)
    chosen = slot_map == column - jnp.floor((column + 0.5) * (1.0 / slots)) * slots
    pick[...] = jnp.where(chosen, 1.0, 0.0).astype(bf16).T
    mix[...] = jnp.where(chosen, weight_map, 0.0).astype(bf16)

    def to_partner(k):
        @pl.loop(0, pairs)
        def _(j):
            slot = lax.rem(line + j, pairs)
            for i in range(1, sections):
                plane_copy(k, i, lax.rem(section + i, sections), slot).wait_recv()

        pair_copy(k, core).start()

    to_partner(0)
    for k in range(out_chunks):
        if k + 1 < out_chunks:
            to_partner(k + 1)
        pair_copy(k, 1 - core).wait_recv()
        block = rows_all[k].astype(f32).reshape(rows, out_span).astype(bf16)
        packed[...] = jnp.dot(pick[...], block, preferred_element_type=f32).astype(bf16)
        for e in range(local):
            if k == 0:
                up_copy(e).wait()
            held = slice(e * slots, (e + 1) * slots)
            both = lax.dot_general(
                packed[held, :],
                w_up[e, :, :, k * out_span : (k + 1) * out_span].reshape(2 * units, out_span),
                flat,
                preferred_element_type=f32,
            )
            if k > 0:
                both = both + lifted[held, :]
            if k + 1 < out_chunks:
                lifted[held, :] = both
            else:
                gate, lift = both[:, :units], both[:, units:]
                activated[held, :] = (gate / (1.0 + jnp.exp(-gate)) * lift).astype(bf16)

    def back_pair_copy(k):
        return remote(
            sum_out.at[k], pair_in.at[k], back_pair_send.at[k], back_pair_recv.at[k], partner
        )

    def back_plane_copy(k, i, landing, slot):
        t = lax.rem(section + i, sections)
        return remote(
            pair_sum.at[k, t, slot],
            plane_in.at[k, landing, slot],
            back_plane_send.at[k, i, slot],
            back_plane_recv.at[k, landing, slot],
            (t, dev),
        )

    def back_line_copy(k, i, landing):
        t = lax.rem(line + i, pairs)
        return remote(
            plane_sum.at[k, t],
            line_in.at[k, landing],
            back_line_send.at[k, i],
            back_line_recv.at[k, landing],
            (section, 2 * t + core),
        )

    def done_copy(k, i, landing):
        return remote(
            own_out.at[k],
            finished.at[k, landing],
            done_send.at[k, i],
            done_recv.at[k, landing],
            (lax.rem(section + i, sections), dev),
        )

    def over_plane(k):
        back_pair_copy(k).wait_recv()
        pair_sum[k] = (pair_sum[k].astype(f32) + pair_in[k].astype(f32)).astype(bf16)

        @pl.loop(1, pairs)
        def _(j):
            for i in range(1, sections):
                back_plane_copy(k, i, section, lax.rem(line + j, pairs)).start()

    def plane_total(k, slot):
        added = pair_sum[k, section, slot].astype(f32)
        for i in range(1, sections):
            t = lax.rem(section + i, sections)
            back_plane_copy(k, i, t, slot).wait_recv()
            added = added + plane_in[k, t, slot].astype(f32)
        return added

    def over_line(k):
        @pl.loop(1, pairs)
        def _(j):
            slot = lax.rem(line + j, pairs)
            plane_sum[k, slot] = plane_total(k, slot).astype(bf16)
            back_line_copy(k, j, line).start()

    def over_sections(k):
        result = middle[:, k * span : (k + 1) * span] + plane_total(k, line)
        for i in range(1, pairs):
            slot = lax.rem(line + i, pairs)
            back_line_copy(k, i, slot).wait_recv()
            result = result + line_in[k, slot].astype(f32)
        own_out[k] = result.astype(bf16)
        finished[k, section] = result.astype(bf16)
        for i in range(1, sections):
            done_copy(k, i, section).start()

    for k in range(chunks):
        part_of = slice(k * span, (k + 1) * span)
        outs = []
        for e in range(local):
            if k == 0:
                down_copy(e).wait()
            held = slice(e * slots, (e + 1) * slots)
            outs.append(
                jnp.dot(
                    activated[held, :], w_down[e, :, part_of], preferred_element_type=f32
                ).astype(bf16)
            )
        routed = jnp.concatenate(outs, axis=0)

        def mixed_rows(which):
            held = pl.ds(pl.multiple_of(which * (rows // 2), rows // 2), rows // 2)
            mixed = jnp.dot(mix[held, :], routed, preferred_element_type=f32)
            return mixed.reshape(sections, pairs, quarter, span)

        sum_out[k] = mixed_rows(1 - core).astype(bf16)
        back_pair_copy(k).start()
        pair_sum[k] = mixed_rows(core).astype(bf16)
        if k > 0:
            over_plane(k - 1)
    over_plane(chunks - 1)
    for k in range(chunks):
        for i in range(1, sections):
            back_plane_copy(k, i, section, line).start()
    for k in range(chunks):
        over_line(k)
    for k in range(chunks):
        over_sections(k)

    def finish_copy(k):
        return pltpu.make_async_copy(
            finished.at[k], out_ref.at[:, :, pl.ds(k * span, span)], finish_sem.at[k]
        )

    for k in range(chunks):
        for i in range(1, sections):
            done_copy(k, i, lax.rem(section + i, sections)).wait_recv()
        finish_copy(k).start()

    for i in range(1, sections):
        part_copy(i, section).wait_send()

    @pl.loop(1, total)
    def _(i):
        table_copy(i, here).wait_send()

    for k in range(out_chunks):

        @pl.loop(1, pairs)
        def _(i):
            line_copy(k, i, line).wait_send()

        @pl.loop(0, pairs)
        def _(j):
            for i in range(1, sections):
                plane_copy(k, i, section, j).wait_send()

        pair_copy(k, core).wait_send()

    for k in range(chunks):

        @pl.loop(1, pairs)
        def _(i):
            back_line_copy(k, i, line).wait_send()

        @pl.loop(0, pairs)
        def _(j):
            for i in range(1, sections):
                back_plane_copy(k, i, section, j).wait_send()

        for i in range(1, sections):
            done_copy(k, i, section).wait_send()
        back_pair_copy(k).wait_send()
        finish_copy(k).wait()


def per_device(
    hidden,
    lengths,
    attn_gain,
    w_query,
    w_latent,
    latent_gain,
    w_rope_key,
    w_key_up,
    w_value_up,
    w_out,
    latent_cache,
    rope_cache,
    ffn_gain,
    expert_ids,
    route_weights,
    w_gate_up,
    w_down,
):
    sections = lax.axis_size("section")
    devices = lax.axis_size("dev")
    total = sections * devices
    pairs = devices // 2
    row_count, width = hidden.shape
    quarter = row_count // sections
    heads, latent, _ = w_key_up.shape
    rope, slots_kept = rope_cache.shape[1:]
    local, _, units, _ = w_gate_up.shape
    experts = local * devices
    slots = total * MOST
    rows = total * quarter
    out_chunks, chunks = OUT_CHUNKS, BACK_CHUNKS
    out_span, span = width // out_chunks, width // chunks
    groups = CACHE_GROUPS
    padded = -(-heads // 8) * 8
    bf16, f32 = jnp.bfloat16, jnp.float32
    anywhere = pl.BlockSpec(memory_space=pl.ANY)
    sems = lambda *count: pltpu.SemaphoreType.DMA(count)
    out = pl.pallas_call(
        functools.partial(layer_kernel, sections, devices),
        out_shape=jax.ShapeDtypeStruct((sections, quarter, width), bf16),
        in_specs=[anywhere] * 17,
        out_specs=anywhere,
        scratch_shapes=[
            pltpu.SMEM(lengths.shape, jnp.int32),
            pltpu.SMEM(expert_ids.shape[::-1], jnp.int32),
            pltpu.SMEM(route_weights.shape[::-1], f32),
            pltpu.VMEM(hidden.shape, bf16),
            pltpu.VMEM((1, width), f32),
            pltpu.VMEM((1, latent), f32),
            pltpu.VMEM((1, width), f32),
            pltpu.VMEM(w_query.shape, bf16),
            pltpu.VMEM(w_latent.shape, bf16),
            pltpu.VMEM(w_rope_key.shape, bf16),
            pltpu.VMEM(w_key_up.shape, bf16),
            pltpu.VMEM(w_value_up.shape, bf16),
            pltpu.VMEM(w_out.shape, bf16),
            pltpu.VMEM(latent_cache.shape, bf16),
            pltpu.VMEM(rope_cache.shape, bf16),
            pltpu.VMEM((row_count, width), f32),
            pltpu.VMEM((row_count, padded, latent), f32),
            pltpu.VMEM((row_count, padded, rope), f32),
            pltpu.VMEM((row_count * padded, 128), f32),
            pltpu.VMEM((row_count * padded, slots_kept), f32),
            pltpu.VMEM((row_count, padded, latent), f32),
            pltpu.VMEM((sections, quarter, width), bf16),
            pltpu.VMEM(w_gate_up.shape, bf16),
            pltpu.VMEM(w_down.shape, bf16),
            pltpu.VMEM((sections, quarter, width), bf16),
            pltpu.VMEM((quarter, width), f32),
            pltpu.VMEM((quarter, 2 * experts), f32),
            pltpu.VMEM((total, quarter, 2 * experts), f32),
            pltpu.VMEM((out_chunks, quarter, out_span), bf16),
            pltpu.VMEM((out_chunks, 2, sections, pairs, quarter, out_span), bf16),
            pltpu.VMEM((local * slots, rows), bf16),
            pltpu.VMEM((rows, local * slots), bf16),
            pltpu.VMEM((local * slots, out_span), bf16),
            pltpu.VMEM((local * slots, 2 * units), f32),
            pltpu.VMEM((local * slots, units), bf16),
            pltpu.VMEM((chunks, sections, pairs, quarter, span), bf16),
            pltpu.VMEM((chunks, sections, pairs, quarter, span), bf16),
            pltpu.VMEM((chunks, sections, pairs, quarter, span), bf16),
            pltpu.VMEM((chunks, sections, pairs, quarter, span), bf16),
            pltpu.VMEM((chunks, pairs, quarter, span), bf16),
            pltpu.VMEM((chunks, pairs, quarter, span), bf16),
            pltpu.VMEM((chunks, quarter, span), bf16),
            pltpu.VMEM((chunks, sections, quarter, span), bf16),
            sems(13),
            sems(2 * groups),
            sems(local),
            sems(local),
            sems(sections),
            sems(sections),
            sems(total),
            sems(total),
            sems(out_chunks, pairs),
            sems(out_chunks, pairs),
            sems(out_chunks, sections, pairs),
            sems(out_chunks, sections, pairs),
            sems(out_chunks),
            sems(out_chunks),
            sems(chunks),
            sems(chunks),
            sems(chunks, sections, pairs),
            sems(chunks, sections, pairs),
            sems(chunks, pairs),
            sems(chunks, pairs),
            sems(chunks, sections),
            sems(chunks, sections),
            sems(chunks),
        ],
        compiler_params=pltpu.CompilerParams(
            collective_id=0, has_side_effects=True, vmem_limit_bytes=63 * 1024 * 1024
        ),
    )(
        lengths,
        expert_ids.T,
        route_weights.T,
        hidden,
        attn_gain.reshape(1, width),
        latent_gain.reshape(1, latent),
        ffn_gain.reshape(1, width),
        w_query,
        w_latent,
        w_rope_key,
        w_key_up,
        w_value_up,
        w_out,
        latent_cache,
        rope_cache,
        w_gate_up,
        w_down,
    )
    return out.reshape(row_count, width)


def solution(mesh):
    in_specs = (
        P("dev", None),
        P("dev"),
        P(),
        P(None, "section"),
        P(),
        P(),
        P(),
        P("section", None, None),
        P("section", None, None),
        P("section", None),
        P("dev", None, None),
        P("dev", None, None),
        P(),
        P("dev", None),
        P("dev", None),
        P("dev", None, "section", None),
        P("dev", "section", None),
    )
    out_specs = P("dev", None)
    return jax.shard_map(
        per_device, mesh=mesh, in_specs=in_specs, out_specs=out_specs, check_vma=False
    )
```
